128 devices in a mesh: row: 64 (over z, y, x), col: 2 (over core).
Axes of the slice: x: 4, y: 4, z: 4, core: 2. Of those that a mesh axis runs over, the one named last changes fastest.
Arguments:
- queries: bfloat16 [65536, 1024], P(('row', 'col')), may hold values from -150 to 150
- keys: bfloat16 [65536, 128], P(('col', 'row')), may hold values from -6.1 to 6.1
- values: bfloat16 [65536, 128], P(('col', 'row')), may hold values from -6 to 6
- row_ptr: int32 [513], replicated, may hold values from 0 to 8192, as said below
- col_blocks: int32 [8192], replicated, may hold values from 0 to 511, as said below
- w_out: bfloat16 [1024, 8192], replicated, may hold values from -0.1875 to 0.1875
Outputs:
- projected: bfloat16 [65536, 8192], P(('row', 'col'))
The draws below stay inside these ranges and needn't reach their ends.
Inputs may be any that keep to these rules, and one draw needn't show every extreme that they name: row_ptr[0] is 0 and row_ptr never falls; block-row b lists row_ptr[b+1] - row_ptr[b] blocks, 1 to 31; row_ptr[g * 8] = g * 8 * 16 for every g; in every group of 8 consecutive block-rows some block-row lists exactly 31 blocks. col_blocks[e] lies in key group e mod 2, that is between (e mod 2) * 256 and (e mod 2) * 256 + 255; the blocks listed for one block-row are distinct.
All inputs are finite; a program needn't handle non-finite values.
Results may differ from the reference program's by a relative error of at most 0.0055.
Values may be sent and summed in bfloat16 or wider, within the bound.
No kernel may reach another device: no remote copies, remote signals or barrier semaphores. Data moves between devices by JAX's collectives and lax.ppermute only.
A program may use at most 192 MiB of HBM per device.

```python
import jax
import jax.numpy as jnp
from jax import lax

D = 8192
HEADS = 8
HEAD_DIM = 128
BLOCK = 128
RPD = 8
AVG = 16
MOST = 31
NB = 512
SEQ = 65536
NNZ = 8192
ROW_GROUPS = 64
KEY_GROUPS = 2
GROUP_BLOCKS = 256


def pattern(key):
    pattern_key = jax.random.fold_in(key, 7001)
    order_key, length_key, rotate_key = jax.random.split(pattern_key, 3)
    ranking = jax.random.randint(order_key, (ROW_GROUPS, RPD), 0, 1 << 20) * RPD + jnp.arange(RPD, dtype=jnp.int32)[None, :]
    ordering = jnp.argsort(ranking, axis=1, stable=True)
    position = jnp.argsort(ordering, axis=1, stable=True)
    pair_count = RPD // 2
    first_half = jax.random.randint(length_key, (ROW_GROUPS, pair_count), 1, 2 * AVG)
    first_half = jnp.where(jnp.arange(pair_count)[None, :] == 0, MOST, first_half)
    paired = jnp.stack([first_half, 2 * AVG - first_half], axis=2).reshape(ROW_GROUPS, RPD)
    lengths = jnp.take_along_axis(paired, position, axis=1).reshape(NB).astype(jnp.int32)
    row_ptr = jnp.concatenate([jnp.zeros((1,), jnp.int32), jnp.cumsum(lengths).astype(jnp.int32)])
    entry_ids = jnp.arange(NNZ, dtype=jnp.int32)
    owners = jnp.clip(jnp.searchsorted(row_ptr, entry_ids, side='right') - 1, 0, NB - 1).astype(jnp.int32)
    group_ids = entry_ids % KEY_GROUPS
    rotation = jax.random.randint(rotate_key, (NB, KEY_GROUPS), 0, GROUP_BLOCKS)
    offsets = (rotation[owners, group_ids] + entry_ids // KEY_GROUPS) % GROUP_BLOCKS
    col_blocks = (group_ids * GROUP_BLOCKS + offsets).astype(jnp.int32)
    return (row_ptr, col_blocks)


def make_keys(key):
    drawn = jax.random.truncated_normal(jax.random.fold_in(key, 7002), -6.0, 6.0, (SEQ, HEAD_DIM), jnp.float32)
    return drawn


def draw_row_ptr(key, part):
    return pattern(key)[0]


def draw_col_blocks(key, part):
    return pattern(key)[1]


def draw_keys(key, part):
    return make_keys(key).astype(jnp.bfloat16)


def draw_queries(key, part):
    drawn = jax.random.truncated_normal(jax.random.fold_in(key, 7003), -6.0, 6.0, (SEQ, HEADS * HEAD_DIM), jnp.float32)
    return drawn.astype(jnp.bfloat16)


def block_levels(key, dims, cuts, low, high):
    gain, own = 1.0, jax.random.fold_in(key, 6)
    for dim, blocks in cuts:
        draws = jnp.exp(jax.random.uniform(jax.random.fold_in(own, dim), (blocks,), jnp.float32, low / len(cuts), high / len(cuts)))
        gain = gain * jnp.repeat(draws, dims[dim] // blocks).reshape([-1 if axis == dim else 1 for axis in range(len(dims))])
    return gain


def normal_values(rng, shape, deviation, reach, shards=(), kind=jnp.bfloat16):
    array = deviation * jax.random.normal(rng, shape, jnp.float32)
    if shards:
        array = array * block_levels(rng, shape, shards, -0.22, 0.18)
    return jnp.clip(array, -reach, reach).astype(kind)


def setup_inputs(seed: int = 0) -> dict:
    streams_of = jax.random.split(jax.random.key(seed), 7)
    queries = draw_queries(jax.random.fold_in(streams_of[6], 71), 0)
    keys = draw_keys(jax.random.fold_in(streams_of[6], 71), 0)
    values = normal_values(streams_of[2], (SEQ, HEAD_DIM), 1.0, 6.0, ((0, 128),))
    row_ptr = draw_row_ptr(jax.random.fold_in(streams_of[6], 71), 0)
    col_blocks = draw_col_blocks(jax.random.fold_in(streams_of[6], 71), 0)
    w_out = normal_values(streams_of[5], (HEADS * HEAD_DIM, D), (HEADS * HEAD_DIM) ** -0.5, 0.1875)
    return dict(queries=queries, keys=keys, values=values, row_ptr=row_ptr, col_blocks=col_blocks, w_out=w_out)


def entry_terms(query_tile, key_tile, value_tile):
    query_heads = query_tile.reshape(BLOCK, HEADS, HEAD_DIM).astype(jnp.float32)
    key_rows = key_tile.astype(jnp.float32)
    value_rows = value_tile.astype(jnp.float32)
    scores = jnp.einsum("qhd,kd->hqk", query_heads, key_rows) * (HEAD_DIM ** -0.5)
    maxima = jnp.max(scores, axis=2)
    exp_scores = jnp.exp(scores - maxima[:, :, None])
    weight_sums = jnp.sum(exp_scores, axis=2)
    weights = exp_scores.astype(jnp.bfloat16).astype(jnp.float32)
    partial_value = jnp.einsum("hqk,kd->qhd", weights, value_rows)
    return maxima.T, weight_sums.T, partial_value


def reference(queries, keys, values, row_ptr, col_blocks, w_out):
    entry_ids = jnp.arange(NNZ, dtype=jnp.int32)
    owners = (jnp.searchsorted(row_ptr, entry_ids, side="right") - 1).astype(jnp.int32)
    initial = (jnp.full((NB, BLOCK, HEADS), -1e30, jnp.float32),
               jnp.zeros((NB, BLOCK, HEADS), jnp.float32),
               jnp.zeros((NB, BLOCK, HEADS, HEAD_DIM), jnp.float32))

    def absorb(running, entry):
        run_max, run_sum, run_out = running
        row_id, col_id = entry
        query_tile = lax.dynamic_slice_in_dim(queries, (row_id * BLOCK).astype(jnp.int32), BLOCK, 0)
        key_tile = lax.dynamic_slice_in_dim(keys, (col_id * BLOCK).astype(jnp.int32), BLOCK, 0)
        value_tile = lax.dynamic_slice_in_dim(values, (col_id * BLOCK).astype(jnp.int32), BLOCK, 0)
        maxima, weight_sums, partial_value = entry_terms(query_tile, key_tile, value_tile)
        old_max = run_max[row_id]
        new_max = jnp.maximum(old_max, maxima)
        keep_old = jnp.exp(old_max - new_max)
        keep_new = jnp.exp(maxima - new_max)
        new_sum = run_sum[row_id] * keep_old + weight_sums * keep_new
        new_out = run_out[row_id] * keep_old[..., None] + partial_value * keep_new[..., None]
        return (run_max.at[row_id].set(new_max), run_sum.at[row_id].set(new_sum),
                run_out.at[row_id].set(new_out)), None

    final, unused = lax.scan(absorb, initial, (owners, col_blocks))
    attention = (final[2] / final[1][..., None]).astype(jnp.bfloat16).reshape(NB, BLOCK, HEADS * HEAD_DIM)

    def project(tile_rows):
        return jnp.dot(tile_rows, w_out, preferred_element_type=jnp.float32).astype(jnp.bfloat16)

    return lax.map(project, attention).reshape(SEQ, D)
```

```python
import functools

import jax
import jax.numpy as jnp
from jax import lax
from jax.experimental import pallas as pl
from jax.experimental.pallas import tpu as pltpu
from jax.sharding import PartitionSpec as P

HEADS = 8
HEAD_DIM = 128
BLOCK = 128
RPD = 8
AVG = 16
MOST = 31
SHARD = 512
BIG = 688
SMALL = 2 * SHARD - BIG
SPLIT = BIG - SHARD - BLOCK
SLOTS = 64
PAIRS = 8
SCALE = 1.4426950408889634 * HEAD_DIM ** (-0.5)
STRIDE = {"x": 1, "y": 4, "z": 16}
BIG_AXES = ("yzx", "xyz")
SMALL_AXES = ("zxy", "zxy")


def send(array, axes, place):
    pairs = []
    for row in range(64):
        for core in range(2):
            stride = STRIDE[axes[core]]
            at = (row // stride) % 4
            pairs.append((row * 2 + core, (row + (place(at) - at) * stride) * 2 + core))
    return lax.ppermute(array, ("row", "col"), pairs)


def swap(array):
    pairs = [(row * 2 + core, row * 2 + 1 - core) for row in range(64) for core in range(2)]
    return lax.ppermute(array, ("row", "col"), pairs)


def doubled(array, axes):
    array = jnp.concatenate([array, send(array, axes, lambda at: at ^ 1)], axis=0)
    return jnp.concatenate([array, send(array, axes, lambda at: 3 - at)], axis=0)


def ring(array, axes):
    half = array.shape[0] // 2
    after = send(array, axes, lambda at: (at + 3) % 4)
    before = send(array, axes, lambda at: (at + 1) % 4)
    low = send(after[:half], axes, lambda at: (at + 3) % 4)
    high = send(before[half:], axes, lambda at: (at + 1) % 4)
    return jnp.concatenate([array, after, before, low, high], axis=0)


def gathered(part, axes):
    first, second, third = ([axes[core][phase] for core in range(2)] for phase in range(3))
    tiles = part.reshape(-1, 8, HEAD_DIM)
    tiles = doubled(tiles, first)
    tiles = ring(tiles, second)
    tiles = ring(tiles, third)
    return tiles.reshape(-1, HEAD_DIM)


def gray(number):
    return number ^ (number >> 1)


def slot_of(theirs, mine, axes):
    first, second, third = axes
    return (
        gray(theirs[first] ^ mine[first])
        + 4 * gray((theirs[second] - mine[second]) & 3)
        + 16 * gray((theirs[third] - mine[third]) & 3)
    )


def attend(place, ptr, cols, q_ref, big, small, o_ref, lse_ref, kbuf, vbuf, qs, s_ref, m_ref, acc, ksem, vsem):
    row_pos, core, first_row = place[0], place[1], place[2]
    mine = {axis: (row_pos // STRIDE[axis]) & 3 for axis in "xyz"}

    def start_of(row):
        return (ptr[row] - ptr[0] + 1 - core) >> 1

    base = start_of(first_row)

    def aligned(row):
        return pl.multiple_of(row, 16)

    def copies(index, act):
        slot = index - base
        block = cols[2 * index + core] - 256 * core
        owner, within = block >> 2, block & 3
        theirs = {axis: (owner // STRIDE[axis]) & 3 for axis in "xyz"}
        in_big = jnp.where(
            core == 0, slot_of(theirs, mine, BIG_AXES[0]), slot_of(theirs, mine, BIG_AXES[1])
        )
        in_small = slot_of(theirs, mine, SMALL_AXES[0])
        at = slot * BLOCK

        def copy(source, row, rows, target, to, sem):
            return pltpu.make_async_copy(
                source.at[pl.ds(aligned(row), rows), :],
                target.at[pl.ds(aligned(to), rows), pl.ds(0, HEAD_DIM)],
                sem.at[slot],
            )

        copy(big, in_big * BIG + within * BLOCK, BLOCK, kbuf, at, ksem).start()

        @pl.when(within == 0)
        def _():
            copy(big, in_big * BIG + SHARD, BLOCK, vbuf, at, vsem).start()

        @pl.when(within == 1)
        def _():
            copy(big, in_big * BIG + SHARD + BLOCK, SPLIT, vbuf, at, vsem).start()
            copy(small, in_small * SMALL, BLOCK - SPLIT, vbuf, at + SPLIT, vsem).start()

        @pl.when(within >= 2)
        def _():
            row = in_small * SMALL + (BLOCK - SPLIT) + (within - 2) * BLOCK
            copy(small, row, BLOCK, vbuf, at, vsem).start()

    def issue(index, _):
        copies(index, None)
        return 0

    lax.fori_loop(base, start_of(first_row + 4), issue, 0)
    vbuf[:, HEAD_DIM:] = jnp.ones((SLOTS * BLOCK, HEAD_DIM), jnp.bfloat16)

    def arrived(buf, sem, slot):
        pltpu.make_async_copy(
            big.at[pl.ds(0, BLOCK), :],
            buf.at[pl.ds(aligned(slot * BLOCK), BLOCK), pl.ds(0, HEAD_DIM)],
            sem.at[slot],
        ).wait()

    def scores_of(slot, rows):
        return lax.dot_general(
            qs[...],
            kbuf[pl.ds(aligned(slot * BLOCK), rows), :],
            (((1,), (1,)), ((), ())),
            preferred_element_type=jnp.float32,
        )

    def block_row(local, _):
        row = first_row + local
        begin, end = start_of(row) - base, start_of(row + 1) - base
        pairs = (end - begin) >> 1
        odd = ((end - begin) & 1) == 1
        for head in range(HEADS):
            qs[head * BLOCK : (head + 1) * BLOCK, :] = q_ref[
                pl.ds(aligned(local * BLOCK), BLOCK), head * HEAD_DIM : (head + 1) * HEAD_DIM
            ]
        m_ref[...] = jnp.full(m_ref.shape, -1e30, jnp.float32)
        acc[...] = jnp.zeros(acc.shape, jnp.float32)

        def score_pair(pair, _):
            slot = begin + 2 * pair
            arrived(kbuf, ksem, slot)
            arrived(kbuf, ksem, slot + 1)
            scores = scores_of(slot, 2 * BLOCK)
            s_ref[pair] = scores
            m_ref[...] = jnp.maximum(
                m_ref[...], jnp.maximum(scores[:, :BLOCK], scores[:, BLOCK:])
            )
            return 0

        lax.fori_loop(0, pairs, score_pair, 0)

        @pl.when(odd)
        def _():
            arrived(kbuf, ksem, end - 1)
            scores = scores_of(end - 1, BLOCK)
            s_ref[pairs, :, :BLOCK] = scores
            m_ref[...] = jnp.maximum(m_ref[...], scores)

        m_ref[...] = jnp.broadcast_to(
            jnp.max(m_ref[...], axis=1, keepdims=True) * SCALE, m_ref.shape
        )

        def value_pair(pair, _):
            slot = begin + 2 * pair
            arrived(vbuf, vsem, slot)
            arrived(vbuf, vsem, slot + 1)
            top = m_ref[...]
            weights = jnp.concatenate(
                [
                    jnp.exp2(s_ref[pair, :, :BLOCK] * SCALE - top).astype(jnp.bfloat16),
                    jnp.exp2(s_ref[pair, :, BLOCK:] * SCALE - top).astype(jnp.bfloat16),
                ],
                axis=1,
            )
            acc[...] += jnp.dot(
                weights,
                vbuf[pl.ds(aligned(slot * BLOCK), 2 * BLOCK), :],
                preferred_element_type=jnp.float32,
            )
            return 0

        lax.fori_loop(0, pairs, value_pair, 0)

        @pl.when(odd)
        def _():
            arrived(vbuf, vsem, end - 1)
            weights = jnp.exp2(s_ref[pairs, :, :BLOCK] * SCALE - m_ref[...]).astype(jnp.bfloat16)
            acc[...] += jnp.dot(
                weights,
                vbuf[pl.ds(aligned((end - 1) * BLOCK), BLOCK), :],
                preferred_element_type=jnp.float32,
            )

        lane = lax.broadcasted_iota(jnp.int32, (BLOCK, HEAD_DIM), 1)
        tile = jnp.zeros((BLOCK, HEAD_DIM), jnp.float32)
        for head in range(HEADS):
            rows = slice(head * BLOCK, (head + 1) * BLOCK)
            total = acc[rows, HEAD_DIM:]
            total = jnp.where(total > 0.0, total, 1.0)
            o_ref[pl.ds(aligned(local * BLOCK), BLOCK), head * HEAD_DIM : (head + 1) * HEAD_DIM] = (
                acc[rows, :HEAD_DIM] / total
            ).astype(jnp.bfloat16)
            tile = jnp.where(lane == head, m_ref[rows, :] + jnp.log2(total), tile)
        lse_ref[pl.ds(aligned(local * BLOCK), BLOCK), :] = tile
        return 0

    lax.fori_loop(0, 4, block_row, 0)


def attention_call(place, ptr, cols, queries, big, small):
    rows = queries.shape[0]
    smem = pl.BlockSpec(memory_space=pltpu.SMEM)
    vmem = pl.BlockSpec(memory_space=pltpu.VMEM)
    anywhere = pl.BlockSpec(memory_space=pl.ANY)
    return pl.pallas_call(
        attend,
        name="attend",
        out_shape=(
            jax.ShapeDtypeStruct((rows, HEADS * HEAD_DIM), jnp.bfloat16),
            jax.ShapeDtypeStruct((rows, HEAD_DIM), jnp.float32),
        ),
        in_specs=[smem, smem, smem, vmem, anywhere, anywhere],
        out_specs=(vmem, vmem),
        scratch_shapes=[
            pltpu.VMEM((SLOTS * BLOCK, HEAD_DIM), jnp.bfloat16),
            pltpu.VMEM((SLOTS * BLOCK, 2 * HEAD_DIM), jnp.bfloat16),
            pltpu.VMEM((HEADS * BLOCK, HEAD_DIM), jnp.bfloat16),
            pltpu.VMEM((PAIRS, HEADS * BLOCK, 2 * BLOCK), jnp.float32),
            pltpu.VMEM((HEADS * BLOCK, BLOCK), jnp.float32),
            pltpu.VMEM((HEADS * BLOCK, 2 * HEAD_DIM), jnp.float32),
            pltpu.SemaphoreType.DMA((SLOTS,)),
            pltpu.SemaphoreType.DMA((SLOTS,)),
        ],
        compiler_params=pltpu.CompilerParams(vmem_limit_bytes=30 * 2**20),
    )(place, ptr, cols, queries, big, small)


def project(o_a, lse_a, o_b, lse_b, w_ref, out_ref, att):
    @pl.when(pl.program_id(0) == 0)
    def _():
        a, b = lse_a[...], lse_b[...]
        top = jnp.maximum(a, b)
        wa, wb = jnp.exp2(a - top), jnp.exp2(b - top)
        part = wa / (wa + wb)
        for head in range(HEADS):
            columns = slice(head * HEAD_DIM, (head + 1) * HEAD_DIM)
            share = jnp.broadcast_to(part[:, head : head + 1], (part.shape[0], HEAD_DIM))
            mine = o_a[:, columns].astype(jnp.float32)
            theirs = o_b[:, columns].astype(jnp.float32)
            att[:, columns] = (mine * share + theirs * (1.0 - share)).astype(jnp.bfloat16)

    out_ref[...] = jnp.dot(
        att[...], w_ref[...], preferred_element_type=jnp.float32
    ).astype(jnp.bfloat16)


def projection_call(o_a, lse_a, o_b, lse_b, w_out):
    rows, depth = o_a.shape
    width, tile = w_out.shape[1], 1024
    whole = lambda array: pl.BlockSpec(array.shape, lambda i: (0, 0))
    return pl.pallas_call(
        project,
        name="project",
        grid=(width // tile,),
        out_shape=jax.ShapeDtypeStruct((rows, width), jnp.bfloat16),
        in_specs=[
            whole(o_a),
            whole(lse_a),
            whole(o_b),
            whole(lse_b),
            pl.BlockSpec((depth, tile), lambda i: (0, i)),
        ],
        out_specs=pl.BlockSpec((rows, tile), lambda i: (0, i)),
        scratch_shapes=[pltpu.VMEM((rows, depth), jnp.bfloat16)],
        compiler_params=pltpu.CompilerParams(vmem_limit_bytes=24 * 2**20),
    )(o_a, lse_a, o_b, lse_b, w_out)


def local(queries, keys, values, row_ptr, col_blocks, w_out):
    row_pos = lax.axis_index("row")
    core = lax.axis_index("col")
    both = jnp.concatenate([keys, values], axis=0)
    other_queries = swap(queries)
    big = gathered(both[:BIG], BIG_AXES)
    small = gathered(both[BIG:], SMALL_AXES)
    ptr = lax.dynamic_slice_in_dim(row_ptr, row_pos * RPD, RPD + 1, 0)
    cols = lax.dynamic_slice_in_dim(col_blocks, row_pos * (RPD * AVG), RPD * AVG, 0)
    place = lambda first: jnp.stack([row_pos, core, first]).astype(jnp.int32)
    o_theirs, lse_theirs = attention_call(
        place(4 - 4 * core), ptr, cols, other_queries, big, small
    )
    o_got, lse_got = swap(o_theirs), swap(lse_theirs)
    o_own, lse_own = attention_call(place(4 * core), ptr, cols, queries, big, small)
    return projection_call(o_own, lse_own, o_got, lse_got, w_out)


def solution(mesh):
    in_specs = (
        P(("row", "col"), None),
        P(("col", "row"), None),
        P(("col", "row"), None),
        P(),
        P(),
        P(),
    )
    out_specs = P(("row", "col"), None)
    return jax.shard_map(local, mesh=mesh, in_specs=in_specs, out_specs=out_specs, check_vma=False)
```

```python
import functools

import jax
import jax.numpy as jnp
from jax import lax
from jax.experimental import pallas as pl
from jax.experimental.pallas import tpu as pltpu
from jax.sharding import PartitionSpec as P

HEADS = 8
HEAD_DIM = 128
BLOCK = 128
RPD = 8
AVG = 16
MOST = 31
SHARD = 512
BIG = 688
SMALL = 2 * SHARD - BIG
SPLIT = BIG - SHARD - BLOCK
PAIRS = 8
SLOTS = 64
SCALE = 1.4426950408889634 * HEAD_DIM ** (-0.5)
STRIDE = {"x": 1, "y": 4, "z": 16}
BIG_AXES = ("yzx", "xyz")
SMALL_AXES = ("zxy", "zxy")


def send(array, axes, place):
    pairs = []
    for row in range(64):
        for core in range(2):
            stride = STRIDE[axes[core]]
            at = (row // stride) % 4
            pairs.append((row * 2 + core, (row + (place(at) - at) * stride) * 2 + core))
    return lax.ppermute(array, ("row", "col"), pairs)


def swap(array):
    pairs = [(row * 2 + core, row * 2 + 1 - core) for row in range(64) for core in range(2)]
    return lax.ppermute(array, ("row", "col"), pairs)


def together(*arrays):
    return lax.optimization_barrier(arrays)


def back(array, axes):
    return send(array, axes, lambda at: (at + 3) % 4)


def forth(array, axes):
    return send(array, axes, lambda at: (at + 1) % 4)


def gathered(both):
    big = both[:BIG].reshape(-1, 8, HEAD_DIM)
    small = both[BIG:].reshape(-1, 8, HEAD_DIM)
    big_axes = [[axes[phase] for axes in BIG_AXES] for phase in range(3)]
    small_axes = [[axes[phase] for axes in SMALL_AXES] for phase in range(3)]
    for place in (lambda at: at ^ 1, lambda at: 3 - at):
        more_big, more_small = together(
            send(big, big_axes[0], place), send(small, small_axes[0], place)
        )
        big = jnp.concatenate([big, more_big], axis=0)
        small = jnp.concatenate([small, more_small], axis=0)
    half = big.shape[0] // 2, small.shape[0] // 2
    b, s = big_axes[1], small_axes[1]
    big_after, big_before, small_after, small_before = together(
        back(big, b), forth(big, b), back(small, s), forth(small, s)
    )
    big_low, big_high, small_low, small_high = together(
        back(big_after[: half[0]], b),
        forth(big_before[half[0] :], b),
        back(small_after[: half[1]], s),
        forth(small_before[half[1] :], s),
    )
    b, s = big_axes[2], small_axes[2]
    big_first, big_second, small_first, small_second = together(
        jnp.concatenate([big, big_after], axis=0),
        jnp.concatenate([big_before, big_low, big_high], axis=0),
        jnp.concatenate([small, small_after], axis=0),
        jnp.concatenate([small_before, small_low, small_high], axis=0),
    )
    big_a, big_d, small_a, small_d = together(
        back(big_first, b), forth(big_second, b), back(small_first, s), forth(small_second, s)
    )
    big_b, big_c = back(big_second, b), forth(big_first, b)
    small_b, small_c = back(small_second, s), forth(small_first, s)
    big_low, big_high = back(big_a, b), forth(big_d, b)
    small_low, small_high = back(small_a, s), forth(small_d, s)
    flat = lambda *parts: [part.reshape(-1, HEAD_DIM) for part in parts]
    return (
        flat(big_first, big_second, big_a, big_b, big_c, big_d, big_low, big_high),
        flat(
            small_first, small_second, small_a, small_b, small_c, small_d, small_low, small_high
        ),
    )


def gray(number):
    return number ^ (number >> 1)


def slot_of(theirs, mine, axes):
    first, second, third = axes
    return (
        gray(theirs[first] ^ mine[first])
        + 4 * gray((theirs[second] - mine[second]) & 3)
        + 16 * gray((theirs[third] - mine[third]) & 3)
    )


def choose(number, count, act):
    def between(low, high):
        if high - low == 1:
            act(low)
        else:
            middle = (low + high) // 2
            pl.when(number < middle)(lambda: between(low, middle))
            pl.when(number >= middle)(lambda: between(middle, high))

    between(0, count)


def attend(place, ptr, cols, q_ref, *refs):
    big, small = refs[:8], refs[8:16]
    o_ref, lse_ref, kbuf, vbuf, qs, s_ref, m_ref, acc, ksem, vsem = refs[16:]
    row_pos, core, first_row = place[0], place[1], place[2]
    mine = {axis: (row_pos // STRIDE[axis]) & 3 for axis in "xyz"}

    def start_of(row):
        return (ptr[row] - ptr[0] + 1 - core) >> 1

    base = start_of(first_row)

    def aligned(row):
        return pl.multiple_of(row, 16)

    def issue(index, _):
        slot = index - base
        block = cols[2 * index + core] - 256 * core
        owner, within = block >> 2, block & 3
        theirs = {axis: (owner // STRIDE[axis]) & 3 for axis in "xyz"}
        in_big = jnp.where(
            core == 0, slot_of(theirs, mine, BIG_AXES[0]), slot_of(theirs, mine, BIG_AXES[1])
        )
        in_small = slot_of(theirs, mine, SMALL_AXES[0])
        at = slot * BLOCK

        def copy(source, row, rows, target, to, sem):
            pltpu.make_async_copy(
                source.at[pl.ds(aligned(row), rows), :],
                target.at[pl.ds(aligned(to), rows), pl.ds(0, HEAD_DIM)],
                sem.at[slot],
            ).start()

        def from_big(piece):
            row = (in_big & 7) * BIG
            copy(big[piece], row + within * BLOCK, BLOCK, kbuf, at, ksem)

            @pl.when(within == 0)
            def _():
                copy(big[piece], row + SHARD, BLOCK, vbuf, at, vsem)

            @pl.when(within == 1)
            def _():
                copy(big[piece], row + SHARD + BLOCK, SPLIT, vbuf, at, vsem)

        choose(in_big >> 3, 8, from_big)

        def from_small(piece):
            row = (in_small & 7) * SMALL

            @pl.when(within == 1)
            def _():
                copy(small[piece], row, BLOCK - SPLIT, vbuf, at + SPLIT, vsem)

            @pl.when(within >= 2)
            def _():
                copy(small[piece], row + BLOCK - SPLIT + (within - 2) * BLOCK, BLOCK, vbuf, at, vsem)

        pl.when(within >= 1)(lambda: choose(in_small >> 3, 8, from_small))
        return 0

    lax.fori_loop(base, start_of(first_row + 4), issue, 0)
    vbuf[:, HEAD_DIM:] = jnp.ones((SLOTS * BLOCK, HEAD_DIM), jnp.bfloat16)

    def arrived(buf, sem, slot):
        pltpu.make_async_copy(
            big[0].at[pl.ds(0, BLOCK), :],
            buf.at[pl.ds(aligned(slot * BLOCK), BLOCK), pl.ds(0, HEAD_DIM)],
            sem.at[slot],
        ).wait()

    def scores_of(slot, rows):
        return lax.dot_general(
            qs[...],
            kbuf[pl.ds(aligned(slot * BLOCK), rows), :],
            (((1,), (1,)), ((), ())),
            preferred_element_type=jnp.float32,
        )

    def block_row(local, _):
        row = first_row + local
        begin, end = start_of(row) - base, start_of(row + 1) - base
        pairs = (end - begin) >> 1
        odd = ((end - begin) & 1) == 1
        for head in range(HEADS):
            qs[head * BLOCK : (head + 1) * BLOCK, :] = q_ref[
                pl.ds(aligned(local * BLOCK), BLOCK), head * HEAD_DIM : (head + 1) * HEAD_DIM
            ]
        m_ref[...] = jnp.full(m_ref.shape, -1e30, jnp.float32)
        acc[...] = jnp.zeros(acc.shape, jnp.float32)

        def score_pair(pair, _):
            slot = begin + 2 * pair
            arrived(kbuf, ksem, slot)
            arrived(kbuf, ksem, slot + 1)
            scores = scores_of(slot, 2 * BLOCK)
            s_ref[pair] = scores
            m_ref[...] = jnp.maximum(
                m_ref[...], jnp.maximum(scores[:, :BLOCK], scores[:, BLOCK:])
            )
            return 0

        lax.fori_loop(0, pairs, score_pair, 0)

        @pl.when(odd)
        def _():
            arrived(kbuf, ksem, end - 1)
            scores = scores_of(end - 1, BLOCK)
            s_ref[pairs, :, :BLOCK] = scores
            m_ref[...] = jnp.maximum(m_ref[...], scores)

        m_ref[...] = jnp.broadcast_to(
            jnp.max(m_ref[...], axis=1, keepdims=True) * SCALE, m_ref.shape
        )

        def value_pair(pair, _):
            slot = begin + 2 * pair
            arrived(vbuf, vsem, slot)
            arrived(vbuf, vsem, slot + 1)
            top = m_ref[...]
            weights = jnp.concatenate(
                [
                    jnp.exp2(s_ref[pair, :, :BLOCK] * SCALE - top).astype(jnp.bfloat16),
                    jnp.exp2(s_ref[pair, :, BLOCK:] * SCALE - top).astype(jnp.bfloat16),
                ],
                axis=1,
            )
            acc[...] += jnp.dot(
                weights,
                vbuf[pl.ds(aligned(slot * BLOCK), 2 * BLOCK), :],
                preferred_element_type=jnp.float32,
            )
            return 0

        lax.fori_loop(0, pairs, value_pair, 0)

        @pl.when(odd)
        def _():
            arrived(vbuf, vsem, end - 1)
            weights = jnp.exp2(s_ref[pairs, :, :BLOCK] * SCALE - m_ref[...]).astype(jnp.bfloat16)
            acc[...] += jnp.dot(
                weights,
                vbuf[pl.ds(aligned((end - 1) * BLOCK), BLOCK), :],
                preferred_element_type=jnp.float32,
            )

        lane = lax.broadcasted_iota(jnp.int32, (BLOCK, HEAD_DIM), 1)
        tile = jnp.zeros((BLOCK, HEAD_DIM), jnp.float32)
        for head in range(HEADS):
            rows = slice(head * BLOCK, (head + 1) * BLOCK)
            total = acc[rows, HEAD_DIM:]
            total = jnp.where(total > 0.0, total, 1.0)
            o_ref[pl.ds(aligned(local * BLOCK), BLOCK), head * HEAD_DIM : (head + 1) * HEAD_DIM] = (
                acc[rows, :HEAD_DIM] / total
            ).astype(jnp.bfloat16)
            tile = jnp.where(lane == head, m_ref[rows, :] + jnp.log2(total), tile)
        lse_ref[pl.ds(aligned(local * BLOCK), BLOCK), :] = tile
        return 0

    lax.fori_loop(0, 4, block_row, 0)


def attention_call(place, ptr, cols, queries, big, small):
    rows = queries.shape[0]
    smem = pl.BlockSpec(memory_space=pltpu.SMEM)
    vmem = pl.BlockSpec(memory_space=pltpu.VMEM)
    anywhere = pl.BlockSpec(memory_space=pl.ANY)
    return pl.pallas_call(
        attend,
        name="attend",
        out_shape=(
            jax.ShapeDtypeStruct((rows, HEADS * HEAD_DIM), jnp.bfloat16),
            jax.ShapeDtypeStruct((rows, HEAD_DIM), jnp.float32),
        ),
        in_specs=[smem, smem, smem, vmem, *[anywhere] * 16],
        out_specs=(vmem, vmem),
        scratch_shapes=[
            pltpu.VMEM((SLOTS * BLOCK, HEAD_DIM), jnp.bfloat16),
            pltpu.VMEM((SLOTS * BLOCK, 2 * HEAD_DIM), jnp.bfloat16),
            pltpu.VMEM((HEADS * BLOCK, HEAD_DIM), jnp.bfloat16),
            pltpu.VMEM((PAIRS, HEADS * BLOCK, 2 * BLOCK), jnp.float32),
            pltpu.VMEM((HEADS * BLOCK, BLOCK), jnp.float32),
            pltpu.VMEM((HEADS * BLOCK, 2 * HEAD_DIM), jnp.float32),
            pltpu.SemaphoreType.DMA((SLOTS,)),
            pltpu.SemaphoreType.DMA((SLOTS,)),
        ],
        compiler_params=pltpu.CompilerParams(vmem_limit_bytes=20 * 2**20),
    )(place, ptr, cols, queries, *big, *small)


def project(o_a, lse_a, o_b, lse_b, w_ref, out_ref, att):
    @pl.when(pl.program_id(0) == 0)
    def _():
        a, b = lse_a[...], lse_b[...]
        top = jnp.maximum(a, b)
        wa, wb = jnp.exp2(a - top), jnp.exp2(b - top)
        part = wa / (wa + wb)
        for head in range(HEADS):
            columns = slice(head * HEAD_DIM, (head + 1) * HEAD_DIM)
            share = jnp.broadcast_to(part[:, head : head + 1], (part.shape[0], HEAD_DIM))
            mine = o_a[:, columns].astype(jnp.float32)
            theirs = o_b[:, columns].astype(jnp.float32)
            att[:, columns] = (mine * share + theirs * (1.0 - share)).astype(jnp.bfloat16)

    out_ref[...] = jnp.dot(
        att[...], w_ref[...], preferred_element_type=jnp.float32
    ).astype(jnp.bfloat16)


def projection_call(o_a, lse_a, o_b, lse_b, w_out):
    rows, depth = o_a.shape
    width, tile = w_out.shape[1], 1024
    whole = lambda array: pl.BlockSpec(array.shape, lambda i: (0, 0))
    return pl.pallas_call(
        project,
        name="project",
        grid=(width // tile,),
        out_shape=jax.ShapeDtypeStruct((rows, width), jnp.bfloat16),
        in_specs=[
            whole(o_a),
            whole(lse_a),
            whole(o_b),
            whole(lse_b),
            pl.BlockSpec((depth, tile), lambda i: (0, i)),
        ],
        out_specs=pl.BlockSpec((rows, tile), lambda i: (0, i)),
        scratch_shapes=[pltpu.VMEM((rows, depth), jnp.bfloat16)],
        compiler_params=pltpu.CompilerParams(vmem_limit_bytes=24 * 2**20),
    )(o_a, lse_a, o_b, lse_b, w_out)


def local(queries, keys, values, row_ptr, col_blocks, w_out):
    row_pos = lax.axis_index("row")
    core = lax.axis_index("col")
    both = jnp.concatenate([keys, values], axis=0)
    other_queries = swap(queries)
    big, small = gathered(both)
    ptr = lax.dynamic_slice_in_dim(row_ptr, row_pos * RPD, RPD + 1, 0)
    cols = lax.dynamic_slice_in_dim(col_blocks, row_pos * (RPD * AVG), RPD * AVG, 0)
    place = lambda first: jnp.stack([row_pos, core, first]).astype(jnp.int32)
    o_theirs, lse_theirs = attention_call(
        place(4 - 4 * core), ptr, cols, other_queries, big, small
    )
    o_got, lse_got = swap(o_theirs), swap(lse_theirs)
    o_own, lse_own = attention_call(place(4 * core), ptr, cols, queries, big, small)
    return projection_call(o_own, lse_own, o_got, lse_got, w_out)


def solution(mesh):
    in_specs = (
        P(("row", "col"), None),
        P(("col", "row"), None),
        P(("col", "row"), None),
        P(),
        P(),
        P(),
    )
    out_specs = P(("row", "col"), None)
    return jax.shard_map(local, mesh=mesh, in_specs=in_specs, out_specs=out_specs, check_vma=False)
```

```python
import jax
import jax.numpy as jnp
from jax import lax
from jax.experimental import pallas as pl
from jax.experimental.pallas import tpu as pltpu
from jax.sharding import PartitionSpec as P

HEADS = 8
HEAD_DIM = 128
BLOCK = 128
RPD = 8
AVG = 16
SHARD = 512
BIG = 688
SMALL = 2 * SHARD - BIG
SPLIT = BIG - SHARD - BLOCK
QUADS = 4
SLOTS = 64
SCALE = 1.4426950408889634 * HEAD_DIM ** (-0.5)
STRIDE = {"x": 1, "y": 4, "z": 16}
BIG_AXES = ("yzx", "xyz")
SMALL_AXES = ("zxy", "zxy")


def send(array, axes, place):
    pairs = []
    for row in range(64):
        for core in range(2):
            stride = STRIDE[axes[core]]
            at = (row // stride) % 4
            pairs.append((row * 2 + core, (row + (place(at) - at) * stride) * 2 + core))
    return lax.ppermute(array, ("row", "col"), pairs)


def swap(array):
    pairs = [(row * 2 + core, row * 2 + 1 - core) for row in range(64) for core in range(2)]
    return lax.ppermute(array, ("row", "col"), pairs)


def together(*arrays):
    return lax.optimization_barrier(arrays)


def back(array, axes):
    return send(array, axes, lambda at: (at + 3) % 4)


def across(array, axes):
    return send(array, axes, lambda at: (at + 2) % 4)


def forth(array, axes):
    return send(array, axes, lambda at: (at + 1) % 4)


def gathered(both):
    big = both[:BIG].reshape(-1, 8, HEAD_DIM)
    small = both[BIG:].reshape(-1, 8, HEAD_DIM)
    big_axes = [[axes[phase] for axes in BIG_AXES] for phase in range(3)]
    small_axes = [[axes[phase] for axes in SMALL_AXES] for phase in range(3)]
    b, s = big_axes[0], small_axes[0]
    big, *others = together(
        big,
        across(big, b),
        across(small, s),
        back(big, b),
        back(small, s),
        forth(big, b),
        forth(small, s),
    )
    big = jnp.concatenate([big, others[2], others[4], others[0]], axis=0)
    small = jnp.concatenate([small, others[3], others[5], others[1]], axis=0)
    half = big.shape[0] // 2, small.shape[0] // 2
    b, s = big_axes[1], small_axes[1]
    big_after, big_before, small_after, small_before = together(
        back(big, b), forth(big, b), back(small, s), forth(small, s)
    )
    big_low, big_high, small_low, small_high = together(
        back(big_after[: half[0]], b),
        forth(big_before[half[0] :], b),
        back(small_after[: half[1]], s),
        forth(small_before[half[1] :], s),
    )
    b, s = big_axes[2], small_axes[2]
    big_first, big_second, small_first, small_second = together(
        jnp.concatenate([big, big_after], axis=0),
        jnp.concatenate([big_before, big_low, big_high], axis=0),
        jnp.concatenate([small, small_after], axis=0),
        jnp.concatenate([small_before, small_low, small_high], axis=0),
    )
    big_a, big_d, small_a, small_d = together(
        back(big_first, b), forth(big_second, b), back(small_first, s), forth(small_second, s)
    )
    big_b, big_c = back(big_second, b), forth(big_first, b)
    small_b, small_c = back(small_second, s), forth(small_first, s)
    big_low, big_high = back(big_a, b), forth(big_d, b)
    small_low, small_high = back(small_a, s), forth(small_d, s)
    flat = lambda *parts: [
        pltpu.with_memory_space_constraint(part.reshape(-1, HEAD_DIM), pltpu.HBM) for part in parts
    ]
    return (
        flat(big_first, big_second, big_a, big_b, big_c, big_d, big_low, big_high),
        flat(
            small_first, small_second, small_a, small_b, small_c, small_d, small_low, small_high
        ),
    )


def gray(number):
    return number ^ (number >> 1)


def slot_of(theirs, mine, axes):
    first, second, third = axes
    return (
        gray((theirs[first] - mine[first]) & 3)
        + 4 * gray((theirs[second] - mine[second]) & 3)
        + 16 * gray((theirs[third] - mine[third]) & 3)
    )


def choose(number, count, act):
    def between(low, high):
        if high - low == 1:
            act(low)
        else:
            middle = (low + high) // 2
            lax.cond(number < middle, lambda: between(low, middle), lambda: between(middle, high))

    between(0, count)


def aligned(row):
    return pl.multiple_of(row, 16)


def fetch(first_piece, codes, big, small, kbuf, vbuf, sems):
    count = len(big)

    def parts(index):
        code = codes[index]
        in_big, in_small, within = code & 63, (code >> 6) & 63, code >> 12
        return in_big, in_small, within, index * BLOCK

    def has(place):
        piece = (place >> 3) - first_piece
        return (piece >= 0) & (piece < count)

    def copy(source, row, rows, target, to, sem):
        return pltpu.make_async_copy(
            source.at[pl.ds(aligned(row), rows), :], target.at[pl.ds(aligned(to), rows), :], sem
        )

    def issue(index, _):
        in_big, in_small, within, at = parts(index)

        def from_big(piece):
            row = (in_big & 7) * BIG
            copy(big[piece], row + within * BLOCK, BLOCK, kbuf, at, sems.at[0, index]).start()

            @pl.when(within == 0)
            def _():
                copy(big[piece], row + SHARD, BLOCK, vbuf, at, sems.at[1, index]).start()

            @pl.when(within == 1)
            def _():
                copy(big[piece], row + SHARD + BLOCK, SPLIT, vbuf, at, sems.at[1, index]).start()

        def from_small(piece):
            row = (in_small & 7) * SMALL

            @pl.when(within == 1)
            def _():
                copy(small[piece], row, BLOCK - SPLIT, vbuf, at + SPLIT, sems.at[2, index]).start()

            @pl.when(within >= 2)
            def _():
                copy(
                    small[piece],
                    row + BLOCK - SPLIT + (within - 2) * BLOCK,
                    BLOCK,
                    vbuf,
                    at,
                    sems.at[2, index],
                ).start()

        pl.when(has(in_big))(lambda: choose((in_big >> 3) - first_piece, count, from_big))
        pl.when(has(in_small) & (within >= 1))(
            lambda: choose((in_small >> 3) - first_piece, count, from_small)
        )
        return 0

    def finish(index, _):
        in_big, in_small, within, at = parts(index)

        @pl.when(has(in_big))
        def _():
            copy(big[0], 0, BLOCK, kbuf, at, sems.at[0, index]).wait()

            @pl.when(within == 0)
            def _():
                copy(big[0], 0, BLOCK, vbuf, at, sems.at[1, index]).wait()

            @pl.when(within == 1)
            def _():
                copy(big[0], 0, SPLIT, vbuf, at, sems.at[1, index]).wait()

        @pl.when(has(in_small))
        def _():
            @pl.when(within == 1)
            def _():
                copy(small[0], 0, BLOCK - SPLIT, vbuf, at + SPLIT, sems.at[2, index]).wait()

            @pl.when(within >= 2)
            def _():
                copy(small[0], 0, BLOCK, vbuf, at, sems.at[2, index]).wait()

        return 0

    lax.fori_loop(0, SLOTS, issue, 0)
    lax.fori_loop(0, SLOTS, finish, 0)


def fetch_near(codes, *refs):
    fetch(0, codes, refs[:6], refs[6:12], *refs[12:])


def fetch_far(codes, *refs):
    fetch(6, codes, refs[:2], refs[2:4], *refs[6:])


def fetched(codes, big, small):
    vmem = pl.BlockSpec(memory_space=pltpu.VMEM)
    smem = pl.BlockSpec(memory_space=pltpu.SMEM)
    hbm = pl.BlockSpec(memory_space=pltpu.HBM)
    blocks = jax.ShapeDtypeStruct((SLOTS * BLOCK, HEAD_DIM), jnp.bfloat16)
    common = dict(
        out_shape=(blocks, blocks),
        out_specs=(vmem, vmem),
        scratch_shapes=[pltpu.SemaphoreType.DMA((3, SLOTS))],
        compiler_params=pltpu.CompilerParams(vmem_limit_bytes=10 * 2**20),
    )
    near = pl.pallas_call(
        fetch_near, name="fetch_near", in_specs=[smem, *[hbm] * 12], **common
    )(codes, *big[:6], *small[:6])
    return pl.pallas_call(
        fetch_far,
        name="fetch_far",
        in_specs=[smem, *[hbm] * 4, vmem, vmem],
        input_output_aliases={5: 0, 6: 1},
        **common,
    )(codes, *big[6:], *small[6:], *near)


def attend(place, starts, q_ref, kbuf, vbuf, o_ref, stat_ref, s_ref, m_ref, acc):
    first_row = place[0]

    def blocks_of(buf, slot, end, count):
        return [
            buf[pl.ds(aligned(jnp.minimum(slot + k, end - 1) * BLOCK), BLOCK), :]
            for k in range(count)
        ]

    def block_row(local, _):
        row = first_row + local
        begin, end = starts[row], starts[row + 1]
        number = end - begin
        quads = (number + 1) >> 2
        rest = begin + 4 * quads
        m_ref[...] = jnp.full(m_ref.shape, -1e30, jnp.float32)
        acc[...] = jnp.zeros(acc.shape, jnp.float32)

        def score(slot, into, count):
            keys = jnp.concatenate(blocks_of(kbuf, slot, end, count), axis=0)
            heads = jnp.concatenate(
                [
                    q_ref[
                        pl.ds(aligned(local * BLOCK), BLOCK),
                        head * HEAD_DIM : (head + 1) * HEAD_DIM,
                    ]
                    for head in range(HEADS)
                ],
                axis=0,
            )
            scores = lax.dot_general(
                heads, keys, (((1,), (1,)), ((), ())), preferred_element_type=jnp.float32
            )
            columns = [scores[:, k * BLOCK : (k + 1) * BLOCK] for k in range(count)]
            top = m_ref[...]
            for column in columns:
                top = jnp.maximum(top, column)
            m_ref[...] = top
            columns[-1] = jnp.where(slot + count - 1 < end, columns[-1], -1e30)
            for k in range(count):
                s_ref[into, :, k * BLOCK : (k + 1) * BLOCK] = columns[k]

        def weigh(slot, into, count):
            values = jnp.concatenate(blocks_of(vbuf, slot, end, count), axis=0)
            values = jnp.concatenate([values, jnp.ones(values.shape, values.dtype)], axis=1)
            top = m_ref[...]
            weights = jnp.concatenate(
                [
                    jnp.exp2(s_ref[into, :, k * BLOCK : (k + 1) * BLOCK] * SCALE - top).astype(
                        jnp.bfloat16
                    )
                    for k in range(count)
                ],
                axis=1,
            )
            acc[...] += jnp.dot(weights, values, preferred_element_type=jnp.float32)

        def each_quad(step):
            def body(quad, _):
                step(begin + 4 * quad, quad, 4)
                return 0

            lax.fori_loop(0, quads, body, 0)
            pl.when(rest < end)(lambda: step(rest, quads, 2))

        each_quad(score)
        m_ref[...] = jnp.broadcast_to(
            jnp.max(m_ref[...], axis=1, keepdims=True) * SCALE, m_ref.shape
        )
        each_quad(weigh)

        lane = lax.broadcasted_iota(jnp.int32, (BLOCK, HEAD_DIM), 1)
        tops = sums = jnp.zeros((BLOCK, HEAD_DIM), jnp.float32)
        for head in range(HEADS):
            rows = slice(head * BLOCK, (head + 1) * BLOCK)
            o_ref[pl.ds(aligned(local * BLOCK), BLOCK), head * HEAD_DIM : (head + 1) * HEAD_DIM] = (
                acc[rows, :HEAD_DIM].astype(jnp.bfloat16)
            )
            tops = jnp.where(lane == head, m_ref[rows, :], tops)
            sums = jnp.where(lane == head, acc[rows, HEAD_DIM:], sums)
        stat_ref[pl.ds(aligned(local * BLOCK), BLOCK), :HEAD_DIM] = tops
        stat_ref[pl.ds(aligned(local * BLOCK), BLOCK), HEAD_DIM:] = sums
        return 0

    lax.fori_loop(0, 4, block_row, 0)


def attention_call(place, starts, queries, keys, values):
    rows = queries.shape[0]
    smem = pl.BlockSpec(memory_space=pltpu.SMEM)
    vmem = pl.BlockSpec(memory_space=pltpu.VMEM)
    return pl.pallas_call(
        attend,
        name="attend",
        out_shape=(
            jax.ShapeDtypeStruct((rows, HEADS * HEAD_DIM), jnp.bfloat16),
            jax.ShapeDtypeStruct((rows, 2 * HEAD_DIM), jnp.float32),
        ),
        in_specs=[smem, smem, vmem, vmem, vmem],
        out_specs=(vmem, vmem),
        scratch_shapes=[
            pltpu.VMEM((QUADS, HEADS * BLOCK, 4 * BLOCK), jnp.float32),
            pltpu.VMEM((HEADS * BLOCK, BLOCK), jnp.float32),
            pltpu.VMEM((HEADS * BLOCK, 2 * HEAD_DIM), jnp.float32),
        ],
        compiler_params=pltpu.CompilerParams(vmem_limit_bytes=24 * 2**20),
    )(place, starts, queries, keys, values)


def project(o_a, stat_a, o_b, stat_b, w_ref, out_ref, att):
    step, tile = pl.program_id(0), out_ref.shape[1]

    @pl.when(step == 0)
    def _():
        top_a, top_b = stat_a[:, :HEAD_DIM], stat_b[:, :HEAD_DIM]
        top = jnp.maximum(top_a, top_b)
        by_a, by_b = jnp.exp2(top_a - top), jnp.exp2(top_b - top)
        total = stat_a[:, HEAD_DIM:] * by_a + stat_b[:, HEAD_DIM:] * by_b
        by_a, by_b = by_a / total, by_b / total
        for head in range(HEADS):
            columns = slice(head * HEAD_DIM, (head + 1) * HEAD_DIM)
            shape = (att.shape[0], HEAD_DIM)
            part_a = o_a[:, columns].astype(jnp.float32) * jnp.broadcast_to(
                by_a[:, head : head + 1], shape
            )
            part_b = o_b[:, columns].astype(jnp.float32) * jnp.broadcast_to(
                by_b[:, head : head + 1], shape
            )
            att[:, columns] = (part_a + part_b).astype(jnp.bfloat16)

    out_ref[...] = jnp.dot(
        att[...],
        w_ref[:, pl.ds(pl.multiple_of(step * tile, 128), tile)],
        preferred_element_type=jnp.float32,
    ).astype(jnp.bfloat16)


def projection_call(o_a, stat_a, o_b, stat_b, w_out):
    rows, depth = o_a.shape
    width, tile = w_out.shape[1], 1024
    vmem = pl.BlockSpec(memory_space=pltpu.VMEM)
    return pl.pallas_call(
        project,
        name="project",
        grid=(width // tile,),
        out_shape=jax.ShapeDtypeStruct((rows, width), jnp.bfloat16),
        in_specs=[vmem] * 5,
        out_specs=pl.BlockSpec((rows, tile), lambda i: (0, i)),
        scratch_shapes=[pltpu.VMEM((rows, depth), jnp.bfloat16)],
        compiler_params=pltpu.CompilerParams(vmem_limit_bytes=30 * 2**20),
    )(o_a, stat_a, o_b, stat_b, w_out)


def tables(row_pos, core, row_ptr, col_blocks):
    ptr = lax.dynamic_slice_in_dim(row_ptr, row_pos * RPD, RPD + 1, 0)
    cols = lax.dynamic_slice_in_dim(col_blocks, row_pos * (RPD * AVG), RPD * AVG, 0)
    starts = (ptr - row_pos * (RPD * AVG) + 1 - core) >> 1
    halves = cols.reshape(-1, 2)
    block = jnp.where(core == 0, halves[:, 0], halves[:, 1]) - 256 * core
    owner, within = block >> 2, block & 3
    mine = {axis: (row_pos // STRIDE[axis]) & 3 for axis in "xyz"}
    theirs = {axis: (owner // STRIDE[axis]) & 3 for axis in "xyz"}
    in_big = jnp.where(
        core == 0, slot_of(theirs, mine, BIG_AXES[0]), slot_of(theirs, mine, BIG_AXES[1])
    )
    in_small = slot_of(theirs, mine, SMALL_AXES[0])
    return starts.astype(jnp.int32), (in_big | in_small << 6 | within << 12).astype(jnp.int32)


def local(queries, keys, values, row_ptr, col_blocks, w_out):
    row_pos = lax.axis_index("row")
    core = lax.axis_index("col")
    big, small = gathered(jnp.concatenate([keys, values], axis=0))
    other_queries = swap(queries)
    starts, codes = tables(row_pos, core, row_ptr, col_blocks)
    listed = fetched(codes, big, small)
    place = lambda first: first.reshape(1).astype(jnp.int32)
    o_theirs, stat_theirs = attention_call(
        place(4 - 4 * core), starts, other_queries, *listed
    )
    o_got, stat_got = swap(o_theirs), swap(stat_theirs)
    o_own, stat_own = attention_call(place(4 * core), starts, queries, *listed)
    return projection_call(o_own, stat_own, o_got, stat_got, w_out)


def solution(mesh):
    in_specs = (
        P(("row", "col"), None),
        P(("col", "row"), None),
        P(("col", "row"), None),
        P(),
        P(),
        P(),
    )
    out_specs = P(("row", "col"), None)
    return jax.shard_map(local, mesh=mesh, in_specs=in_specs, out_specs=out_specs, check_vma=False)
```

```python
import jax
import jax.numpy as jnp
from jax import lax
from jax.experimental import pallas as pl
from jax.experimental.pallas import tpu as pltpu
from jax.sharding import PartitionSpec as P

HEADS = 8
HEAD_DIM = 128
BLOCK = 128
RPD = 8
AVG = 16
SHARD = 512
BIG = 688
SMALL = 2 * SHARD - BIG
SPLIT = BIG - SHARD - BLOCK
QUADS = 4
NEAR = 7
MERGE = 64
SLOTS = 64
SCALE = 1.4426950408889634 * HEAD_DIM ** (-0.5)
STRIDE = {"x": 1, "y": 4, "z": 16}
BIG_AXES = ("yzx", "xyz")
SMALL_AXES = ("zxy", "zxy")


def send(array, axes, place):
    pairs = []
    for row in range(64):
        for core in range(2):
            stride = STRIDE[axes[core]]
            at = (row // stride) % 4
            pairs.append((row * 2 + core, (row + (place(at) - at) * stride) * 2 + core))
    return lax.ppermute(array, ("row", "col"), pairs)


def swap(array):
    pairs = [(row * 2 + core, row * 2 + 1 - core) for row in range(64) for core in range(2)]
    return lax.ppermute(array, ("row", "col"), pairs)


def together(*arrays):
    return lax.optimization_barrier(arrays)


def back(array, axes):
    return send(array, axes, lambda at: (at + 3) % 4)


def across(array, axes):
    return send(array, axes, lambda at: (at + 2) % 4)


def forth(array, axes):
    return send(array, axes, lambda at: (at + 1) % 4)


def gathered(both):
    big = both[:BIG].reshape(-1, 8, HEAD_DIM)
    small = both[BIG:].reshape(-1, 8, HEAD_DIM)
    big_axes = [[axes[phase] for axes in BIG_AXES] for phase in range(3)]
    small_axes = [[axes[phase] for axes in SMALL_AXES] for phase in range(3)]
    b, s = big_axes[0], small_axes[0]
    big, *others = together(
        big,
        across(big, b),
        across(small, s),
        back(big, b),
        back(small, s),
        forth(big, b),
        forth(small, s),
    )
    big, small = together(
        jnp.concatenate([big, others[2], others[4], others[0]], axis=0),
        jnp.concatenate([small, others[3], others[5], others[1]], axis=0),
    )
    parts = {"big": (big, big_axes), "small": (small, small_axes)}

    def each(act):
        return {part: act(part, parts[part][1][1], parts[part][1][2]) for part in parts}

    def ready(*dicts):
        flat = together(*(array for one in dicts for array in one.values()))
        return [dict(zip(parts, flat[2 * k : 2 * k + 2])) for k in range(len(dicts))]

    joined = lambda *dicts: {
        part: jnp.concatenate([one[part] for one in dicts], axis=0) for part in parts
    }
    own = {part: array for part, (array, _) in parts.items()}
    after = each(lambda part, ring, last: back(own[part], ring))
    before = each(lambda part, ring, last: forth(own[part], ring))
    after, before = ready(after, before)
    half = {part: array.shape[0] // 2 for part, array in own.items()}
    first, before, low, high = ready(
        joined(own, after),
        before,
        {part: after[part][: half[part]] for part in parts},
        {part: before[part][half[part] :] for part in parts},
    )
    low = each(lambda part, ring, last: back(low[part], ring))
    high = each(lambda part, ring, last: forth(high[part], ring))
    first_after = each(lambda part, ring, last: back(first[part], last))
    before_before = each(lambda part, ring, last: forth(before[part], last))
    first_before = each(lambda part, ring, last: forth(first[part], last))
    low, high = ready(low, high)
    rest, second = joined(low, high), joined(before, low, high)
    rest_before = each(lambda part, ring, last: forth(rest[part], last))
    second_after = each(lambda part, ring, last: back(second[part], last))
    before_far = each(lambda part, ring, last: forth(before_before[part], last))
    first_far = each(lambda part, ring, last: back(first_after[part], last))
    rest_far = each(lambda part, ring, last: forth(rest_before[part], last))
    return tuple(
        [
            pltpu.with_memory_space_constraint(piece[part].reshape(-1, HEAD_DIM), pltpu.HBM)
            for piece in (
                first,
                second,
                first_after,
                second_after,
                first_before,
                before_before,
                rest_before,
                first_far,
                before_far,
                rest_far,
            )
        ]
        for part in parts
    )


def gray(number):
    return number ^ (number >> 1)


def slot_of(theirs, mine, axes):
    first, second, third = axes
    return (
        gray((theirs[first] - mine[first]) & 3)
        + 4 * gray((theirs[second] - mine[second]) & 3)
        + 16 * gray((theirs[third] - mine[third]) & 3)
    )


def choose(number, count, act):
    def between(low, high):
        if high - low == 1:
            act(low)
        else:
            middle = (low + high) // 2
            lax.cond(number < middle, lambda: between(low, middle), lambda: between(middle, high))

    between(0, count)


def aligned(row):
    return pl.multiple_of(row, 16)


def fetch(first_piece, codes, big, small, kbuf, vbuf, sems, entries, left=None):
    count = len(big)

    def parts(index):
        code = codes[index]
        big_piece, big_chunk = code & 15, (code >> 4) & 7
        small_piece, small_chunk = (code >> 7) & 15, (code >> 11) & 7
        return big_piece, big_chunk, small_piece, small_chunk, code >> 14, index * BLOCK

    def has(piece):
        return (piece >= first_piece) & (piece < first_piece + count)

    def copy(source, row, rows, target, to, sem):
        return pltpu.make_async_copy(
            source.at[pl.ds(aligned(row), rows), :], target.at[pl.ds(aligned(to), rows), :], sem
        )

    def issue(index):
        big_piece, big_chunk, small_piece, small_chunk, within, at = parts(index)

        def from_big(piece):
            row = big_chunk * BIG
            copy(big[piece], row + within * BLOCK, BLOCK, kbuf, at, sems.at[0, index]).start()

            @pl.when(within == 0)
            def _():
                copy(big[piece], row + SHARD, BLOCK, vbuf, at, sems.at[1, index]).start()

            @pl.when(within == 1)
            def _():
                copy(big[piece], row + SHARD + BLOCK, SPLIT, vbuf, at, sems.at[1, index]).start()

        def from_small(piece):
            row = small_chunk * SMALL

            @pl.when(within == 1)
            def _():
                copy(small[piece], row, BLOCK - SPLIT, vbuf, at + SPLIT, sems.at[2, index]).start()

            @pl.when(within >= 2)
            def _():
                copy(
                    small[piece],
                    row + BLOCK - SPLIT + (within - 2) * BLOCK,
                    BLOCK,
                    vbuf,
                    at,
                    sems.at[2, index],
                ).start()

        pl.when(has(big_piece))(lambda: choose(big_piece - first_piece, count, from_big))
        pl.when(has(small_piece) & (within >= 1))(
            lambda: choose(small_piece - first_piece, count, from_small)
        )

    def finish(index):
        big_piece, _, small_piece, _, within, at = parts(index)

        @pl.when(has(big_piece))
        def _():
            copy(big[1], 0, BLOCK, kbuf, at, sems.at[0, index]).wait()

            @pl.when(within == 0)
            def _():
                copy(big[1], 0, BLOCK, vbuf, at, sems.at[1, index]).wait()

            @pl.when(within == 1)
            def _():
                copy(big[1], 0, SPLIT, vbuf, at, sems.at[1, index]).wait()

        @pl.when(has(small_piece))
        def _():
            @pl.when(within == 1)
            def _():
                copy(small[1], 0, BLOCK - SPLIT, vbuf, at + SPLIT, sems.at[2, index]).wait()

            @pl.when(within >= 2)
            def _():
                copy(small[1], 0, BLOCK, vbuf, at, sems.at[2, index]).wait()

    number, entry_of = entries

    def begin(k, missing):
        index = entry_of(k)
        issue(index)
        if left is None:
            return missing
        big_piece, _, small_piece, _, within, _ = parts(index)
        left[missing] = index
        whole = has(big_piece) & (has(small_piece) | (within == 0))
        return missing + jnp.where(whole, jnp.int32(0), jnp.int32(1))

    missing = lax.fori_loop(0, number, begin, jnp.int32(0))
    if left is not None:
        left[SLOTS] = missing

    def end(k, _):
        finish(entry_of(k))
        return 0

    lax.fori_loop(0, number, end, 0)


def fetch_near(codes, *refs):
    kbuf, vbuf, left, sems = refs[2 * NEAR :]
    fetch(0, codes, refs[:NEAR], refs[NEAR : 2 * NEAR], kbuf, vbuf, sems, (SLOTS, lambda k: k), left)


def fetch_far(codes, left, *refs):
    kbuf, vbuf, sems = refs[8:]
    fetch(NEAR, codes, refs[:3], refs[3:6], kbuf, vbuf, sems, (left[SLOTS], lambda k: left[k]))


def fetched(codes, big, small):
    vmem = pl.BlockSpec(memory_space=pltpu.VMEM)
    smem = pl.BlockSpec(memory_space=pltpu.SMEM)
    hbm = pl.BlockSpec(memory_space=pltpu.HBM)
    blocks = jax.ShapeDtypeStruct((SLOTS * BLOCK, HEAD_DIM), jnp.bfloat16)
    common = dict(
        scratch_shapes=[pltpu.SemaphoreType.DMA((3, SLOTS))],
        compiler_params=pltpu.CompilerParams(vmem_limit_bytes=10 * 2**20),
    )
    *near, left = pl.pallas_call(
        fetch_near,
        name="fetch_near",
        in_specs=[smem, *[hbm] * (2 * NEAR)],
        out_shape=(blocks, blocks, jax.ShapeDtypeStruct((2 * SLOTS,), jnp.int32)),
        out_specs=(vmem, vmem, smem),
        **common,
    )(codes, *big[:NEAR], *small[:NEAR])
    return pl.pallas_call(
        fetch_far,
        name="fetch_far",
        in_specs=[smem, smem, *[hbm] * 6, vmem, vmem],
        out_shape=(blocks, blocks),
        out_specs=(vmem, vmem),
        input_output_aliases={8: 0, 9: 1},
        **common,
    )(codes, left, *big[NEAR:], *small[NEAR:], *near)


def attend(place, starts, q_ref, kbuf, vbuf, o_ref, stat_ref, s_ref, m_ref, acc):
    first_row = place[0]

    def blocks_of(buf, slot, end, count):
        return [
            buf[pl.ds(aligned(jnp.minimum(slot + k, end - 1) * BLOCK), BLOCK), :]
            for k in range(count)
        ]

    def block_row(local, _):
        row = first_row + local
        begin, end = starts[row], starts[row + 1]
        number = end - begin
        quads = (number + 1) >> 2
        rest = begin + 4 * quads
        m_ref[...] = jnp.full(m_ref.shape, -1e30, jnp.float32)
        acc[...] = jnp.zeros(acc.shape, jnp.float32)

        def score(slot, into, count):
            keys = jnp.concatenate(blocks_of(kbuf, slot, end, count), axis=0)
            heads = jnp.concatenate(
                [
                    q_ref[
                        pl.ds(aligned(local * BLOCK), BLOCK),
                        head * HEAD_DIM : (head + 1) * HEAD_DIM,
                    ]
                    for head in range(HEADS)
                ],
                axis=0,
            )
            scores = SCALE * lax.dot_general(
                heads, keys, (((1,), (1,)), ((), ())), preferred_element_type=jnp.float32
            )
            columns = [scores[:, k * BLOCK : (k + 1) * BLOCK] for k in range(count)]
            top = m_ref[...]
            for column in columns:
                top = jnp.maximum(top, column)
            m_ref[...] = top
            columns[-1] = jnp.where(slot + count - 1 < end, columns[-1], -1e30)
            for k in range(count):
                s_ref[into, :, k * BLOCK : (k + 1) * BLOCK] = columns[k]

        def weigh(slot, into, count):
            values = jnp.concatenate(blocks_of(vbuf, slot, end, count), axis=0)
            values = jnp.concatenate([values, jnp.ones(values.shape, values.dtype)], axis=1)
            top = m_ref[...]
            weights = jnp.concatenate(
                [
                    jnp.exp2(s_ref[into, :, k * BLOCK : (k + 1) * BLOCK] - top).astype(
                        jnp.bfloat16
                    )
                    for k in range(count)
                ],
                axis=1,
            )
            acc[...] += jnp.dot(weights, values, preferred_element_type=jnp.float32)

        def each_quad(step):
            def body(quad, _):
                step(begin + 4 * quad, quad, 4)
                return 0

            lax.fori_loop(0, quads, body, 0)
            pl.when(rest < end)(lambda: step(rest, quads, 2))

        each_quad(score)
        m_ref[...] = jnp.broadcast_to(
            jnp.max(m_ref[...], axis=1, keepdims=True), m_ref.shape
        )
        each_quad(weigh)

        lane = lax.broadcasted_iota(jnp.int32, (BLOCK, HEAD_DIM), 1)
        tops = sums = jnp.zeros((BLOCK, HEAD_DIM), jnp.float32)
        for head in range(HEADS):
            rows = slice(head * BLOCK, (head + 1) * BLOCK)
            o_ref[pl.ds(aligned(local * BLOCK), BLOCK), head * HEAD_DIM : (head + 1) * HEAD_DIM] = (
                acc[rows, :HEAD_DIM].astype(jnp.bfloat16)
            )
            tops = jnp.where(lane == head, m_ref[rows, :], tops)
            sums = jnp.where(lane == head, acc[rows, HEAD_DIM:], sums)
        stat_ref[pl.ds(aligned(local * BLOCK), BLOCK), :HEAD_DIM] = tops
        stat_ref[pl.ds(aligned(local * BLOCK), BLOCK), HEAD_DIM:] = sums
        return 0

    lax.fori_loop(0, 4, block_row, 0)


def attention_call(place, starts, queries, keys, values):
    rows = queries.shape[0]
    smem = pl.BlockSpec(memory_space=pltpu.SMEM)
    vmem = pl.BlockSpec(memory_space=pltpu.VMEM)
    return pl.pallas_call(
        attend,
        name="attend",
        out_shape=(
            jax.ShapeDtypeStruct((rows, HEADS * HEAD_DIM), jnp.bfloat16),
            jax.ShapeDtypeStruct((rows, 2 * HEAD_DIM), jnp.float32),
        ),
        in_specs=[smem, smem, vmem, vmem, vmem],
        out_specs=(vmem, vmem),
        scratch_shapes=[
            pltpu.VMEM((QUADS, HEADS * BLOCK, 4 * BLOCK), jnp.float32),
            pltpu.VMEM((HEADS * BLOCK, BLOCK), jnp.float32),
            pltpu.VMEM((HEADS * BLOCK, 2 * HEAD_DIM), jnp.float32),
        ],
        compiler_params=pltpu.CompilerParams(vmem_limit_bytes=24 * 2**20),
    )(place, starts, queries, keys, values)


def project(o_a, stat_a, o_b, stat_b, w_ref, out_ref, att):
    step, tile = pl.program_id(0), out_ref.shape[1]

    def merge(chunk, _):
        rows = pl.ds(aligned(chunk * MERGE), MERGE)
        top_a, top_b = stat_a[rows, :HEAD_DIM], stat_b[rows, :HEAD_DIM]
        top = jnp.maximum(top_a, top_b)
        by_a, by_b = jnp.exp2(top_a - top), jnp.exp2(top_b - top)
        total = stat_a[rows, HEAD_DIM:] * by_a + stat_b[rows, HEAD_DIM:] * by_b
        by_a, by_b = by_a / total, by_b / total
        for head in range(HEADS):
            columns = slice(head * HEAD_DIM, (head + 1) * HEAD_DIM)
            shape = (MERGE, HEAD_DIM)
            part_a = o_a[rows, columns].astype(jnp.float32) * jnp.broadcast_to(
                by_a[:, head : head + 1], shape
            )
            part_b = o_b[rows, columns].astype(jnp.float32) * jnp.broadcast_to(
                by_b[:, head : head + 1], shape
            )
            att[rows, columns] = (part_a + part_b).astype(jnp.bfloat16)
        return 0

    @pl.when(step == 0)
    def _():
        lax.fori_loop(0, att.shape[0] // MERGE, merge, 0)

    out_ref[...] = jnp.dot(
        att[...],
        w_ref[:, pl.ds(pl.multiple_of(step * tile, 128), tile)],
        preferred_element_type=jnp.float32,
    ).astype(jnp.bfloat16)


def projection_call(o_a, stat_a, o_b, stat_b, w_out):
    rows, depth = o_a.shape
    width, tile = w_out.shape[1], 1024
    vmem = pl.BlockSpec(memory_space=pltpu.VMEM)
    return pl.pallas_call(
        project,
        name="project",
        grid=(width // tile,),
        out_shape=jax.ShapeDtypeStruct((rows, width), jnp.bfloat16),
        in_specs=[vmem] * 5,
        out_specs=pl.BlockSpec((rows, tile), lambda i: (0, i)),
        scratch_shapes=[pltpu.VMEM((rows, depth), jnp.bfloat16)],
        compiler_params=pltpu.CompilerParams(vmem_limit_bytes=30 * 2**20),
    )(o_a, stat_a, o_b, stat_b, w_out)


def tables(row_pos, core, row_ptr, col_blocks):
    ptr = lax.dynamic_slice_in_dim(row_ptr, row_pos * RPD, RPD + 1, 0)
    cols = lax.dynamic_slice_in_dim(col_blocks, row_pos * (RPD * AVG), RPD * AVG, 0)
    starts = (ptr - row_pos * (RPD * AVG) + 1 - core) >> 1
    halves = cols.reshape(-1, 2)
    block = jnp.where(core == 0, halves[:, 0], halves[:, 1]) - 256 * core
    owner, within = block >> 2, block & 3
    mine = {axis: (row_pos // STRIDE[axis]) & 3 for axis in "xyz"}
    theirs = {axis: (owner // STRIDE[axis]) & 3 for axis in "xyz"}
    in_big = jnp.where(
        core == 0, slot_of(theirs, mine, BIG_AXES[0]), slot_of(theirs, mine, BIG_AXES[1])
    )
    in_small = slot_of(theirs, mine, SMALL_AXES[0])

    def piece_and_chunk(place):
        plane, inner = place >> 4, place & 15
        halves = 2 * plane + (inner >> 3)
        thirds = 3 * plane - 2 + ((inner - 4) >> 2) * (inner >> 3)
        whole = (plane < 2) | (inner < 8)
        piece = jnp.where(plane < 2, halves, thirds)
        return piece | jnp.where(whole, inner & 7, inner & 3) << 4

    codes = piece_and_chunk(in_big) | piece_and_chunk(in_small) << 7 | within << 14
    return starts.astype(jnp.int32), codes.astype(jnp.int32)


def local(queries, keys, values, row_ptr, col_blocks, w_out):
    row_pos = lax.axis_index("row")
    core = lax.axis_index("col")
    big, small = gathered(jnp.concatenate([keys, values], axis=0))
    other_queries = swap(queries)
    starts, codes = tables(row_pos, core, row_ptr, col_blocks)
    listed = fetched(codes, big, small)
    place = lambda first: first.reshape(1).astype(jnp.int32)
    o_theirs, stat_theirs = attention_call(
        place(4 - 4 * core), starts, other_queries, *listed
    )
    o_got, stat_got = swap(o_theirs), swap(stat_theirs)
    o_own, stat_own = attention_call(place(4 * core), starts, queries, *listed)
    return projection_call(o_own, stat_own, o_got, stat_got, w_out)


def solution(mesh):
    in_specs = (
        P(("row", "col"), None),
        P(("col", "row"), None),
        P(("col", "row"), None),
        P(),
        P(),
        P(),
    )
    out_specs = P(("row", "col"), None)
    return jax.shard_map(local, mesh=mesh, in_specs=in_specs, out_specs=out_specs, check_vma=False)
```

```python
import jax
import jax.numpy as jnp
from jax import lax
from jax.experimental import pallas as pl
from jax.experimental.pallas import tpu as pltpu
from jax.sharding import PartitionSpec as P

HEADS = 8
HEAD_DIM = 128
BLOCK = 128
RPD = 8
AVG = 16
SHARD = 512
BIG = 688
SMALL = 2 * SHARD - BIG
SPLIT = BIG - SHARD - BLOCK
QUADS = 4
NEAR = 7
MERGE = 64
SLOTS = 64
SCALE = 1.4426950408889634 * HEAD_DIM ** (-0.5)
STRIDE = {"x": 1, "y": 4, "z": 16}
BIG_AXES = ("yzx", "xyz")
SMALL_AXES = ("zxy", "zxy")


def send(array, axes, place):
    pairs = []
    for row in range(64):
        for core in range(2):
            stride = STRIDE[axes[core]]
            at = (row // stride) % 4
            pairs.append((row * 2 + core, (row + (place(at) - at) * stride) * 2 + core))
    return lax.ppermute(array, ("row", "col"), pairs)


def swap(array):
    pairs = [(row * 2 + core, row * 2 + 1 - core) for row in range(64) for core in range(2)]
    return lax.ppermute(array, ("row", "col"), pairs)


def together(*arrays):
    return lax.optimization_barrier(arrays)


def back(array, axes):
    return send(array, axes, lambda at: (at + 3) % 4)


def across(array, axes):
    return send(array, axes, lambda at: (at + 2) % 4)


def forth(array, axes):
    return send(array, axes, lambda at: (at + 1) % 4)


def gathered(both):
    def steps(part, axes):
        first, ring, last = ([axes[core][phase] for core in range(2)] for phase in range(3))
        join = lambda *arrays: jnp.concatenate(arrays, axis=0)
        far, after, before = together(across(part, first), back(part, first), forth(part, first))
        (own,) = together(join(part, after, before, far))
        half = own.shape[0] // 2
        after, before = together(back(own, ring), forth(own, ring))
        first_half, before, low, high = together(
            join(own, after), before, after[:half], before[half:]
        )
        low, high = back(low, ring), forth(high, ring)
        first_after, before_before = back(first_half, last), forth(before, last)
        first_before = forth(first_half, last)
        low, high = together(low, high)
        rest, second = join(low, high), join(before, low, high)
        rest_before = forth(rest, last)
        second_after = back(second, last)
        first_far, before_far = back(first_after, last), forth(before_before, last)
        rest_far = forth(rest_before, last)
        pieces = (
            first_half,
            second,
            first_after,
            second_after,
            first_before,
            before_before,
            rest_before,
            first_far,
            before_far,
            rest_far,
        )
        return [
            pltpu.with_memory_space_constraint(piece.reshape(-1, HEAD_DIM), pltpu.HBM)
            for piece in pieces
        ]

    return (
        steps(both[:BIG].reshape(-1, 8, HEAD_DIM), BIG_AXES),
        steps(both[BIG:].reshape(-1, 8, HEAD_DIM), SMALL_AXES),
    )


def gray(number):
    return number ^ (number >> 1)


def slot_of(theirs, mine, axes):
    first, second, third = axes
    return (
        gray((theirs[first] - mine[first]) & 3)
        + 4 * gray((theirs[second] - mine[second]) & 3)
        + 16 * gray((theirs[third] - mine[third]) & 3)
    )


def choose(number, count, act):
    def between(low, high):
        if high - low == 1:
            act(low)
        else:
            middle = (low + high) // 2
            lax.cond(number < middle, lambda: between(low, middle), lambda: between(middle, high))

    between(0, count)


def aligned(row):
    return pl.multiple_of(row, 16)


def fetch(first_piece, codes, big, small, kbuf, vbuf, sems):
    count = len(big)

    def parts(index):
        code = codes[index]
        big_piece, big_chunk = code & 15, (code >> 4) & 7
        small_piece, small_chunk = (code >> 7) & 15, (code >> 11) & 7
        return big_piece, big_chunk, small_piece, small_chunk, code >> 14, index * BLOCK

    def has(piece):
        return (piece >= first_piece) & (piece < first_piece + count)

    def copy(source, row, rows, target, to, sem):
        return pltpu.make_async_copy(
            source.at[pl.ds(aligned(row), rows), :], target.at[pl.ds(aligned(to), rows), :], sem
        )

    def issue(index):
        big_piece, big_chunk, small_piece, small_chunk, within, at = parts(index)

        def from_big(piece):
            row = big_chunk * BIG
            copy(big[piece], row + within * BLOCK, BLOCK, kbuf, at, sems.at[0, index]).start()

            @pl.when(within == 0)
            def _():
                copy(big[piece], row + SHARD, BLOCK, vbuf, at, sems.at[1, index]).start()

            @pl.when(within == 1)
            def _():
                copy(big[piece], row + SHARD + BLOCK, SPLIT, vbuf, at, sems.at[1, index]).start()

        def from_small(piece):
            row = small_chunk * SMALL

            @pl.when(within == 1)
            def _():
                copy(small[piece], row, BLOCK - SPLIT, vbuf, at + SPLIT, sems.at[2, index]).start()

            @pl.when(within >= 2)
            def _():
                copy(
                    small[piece],
                    row + BLOCK - SPLIT + (within - 2) * BLOCK,
                    BLOCK,
                    vbuf,
                    at,
                    sems.at[2, index],
                ).start()

        pl.when(has(big_piece))(lambda: choose(big_piece - first_piece, count, from_big))
        pl.when(has(small_piece) & (within >= 1))(
            lambda: choose(small_piece - first_piece, count, from_small)
        )

    def finish(index):
        big_piece, _, small_piece, _, within, at = parts(index)

        @pl.when(has(big_piece))
        def _():
            copy(big[1], 0, BLOCK, kbuf, at, sems.at[0, index]).wait()

            @pl.when(within == 0)
            def _():
                copy(big[1], 0, BLOCK, vbuf, at, sems.at[1, index]).wait()

            @pl.when(within == 1)
            def _():
                copy(big[1], 0, SPLIT, vbuf, at, sems.at[1, index]).wait()

        @pl.when(has(small_piece))
        def _():
            @pl.when(within == 1)
            def _():
                copy(small[1], 0, BLOCK - SPLIT, vbuf, at + SPLIT, sems.at[2, index]).wait()

            @pl.when(within >= 2)
            def _():
                copy(small[1], 0, BLOCK, vbuf, at, sems.at[2, index]).wait()

    return parts, has, issue, finish


def fetch_near(codes, starts, *refs):
    big, small = refs[:NEAR], refs[NEAR : 2 * NEAR]
    kbuf, vbuf, left, sems = refs[2 * NEAR :]
    parts, has, issue, finish = fetch(0, codes, big, small, kbuf, vbuf, sems)

    def begin(index, missing):
        issue(index)
        big_piece, _, small_piece, _, within, _ = parts(index)
        left[missing] = index
        whole = has(big_piece) & (has(small_piece) | (within == 0))
        return missing + jnp.where(whole, jnp.int32(0), jnp.int32(1))

    def block_row(row, missing):
        missing = lax.fori_loop(starts[row], starts[row + 1], begin, missing)
        left[SLOTS + row] = missing
        return missing

    def end(index, _):
        finish(index)
        return 0

    lax.fori_loop(0, RPD, block_row, jnp.int32(0))
    lax.fori_loop(0, SLOTS, end, 0)


def fetched(codes, starts, big, small):
    vmem = pl.BlockSpec(memory_space=pltpu.VMEM)
    smem = pl.BlockSpec(memory_space=pltpu.SMEM)
    hbm = pl.BlockSpec(memory_space=pltpu.HBM)
    blocks = jax.ShapeDtypeStruct((SLOTS * BLOCK, HEAD_DIM), jnp.bfloat16)
    return pl.pallas_call(
        fetch_near,
        name="fetch_near",
        in_specs=[smem, smem, *[hbm] * (2 * NEAR)],
        out_shape=(blocks, blocks, jax.ShapeDtypeStruct((2 * SLOTS,), jnp.int32)),
        out_specs=(vmem, vmem, smem),
        scratch_shapes=[pltpu.SemaphoreType.DMA((3, SLOTS))],
        compiler_params=pltpu.CompilerParams(vmem_limit_bytes=10 * 2**20),
    )(codes, starts, *big[:NEAR], *small[:NEAR])


def attend(place, starts, codes, left, own_queries, their_queries, *refs):
    big, small = refs[:3], refs[3:6]
    own_out, own_stat, their_out, their_stat, kbuf, vbuf = refs[8:14]
    qs, s_ref, m_ref, acc, sems = refs[14:]
    core = place[0]
    _, _, issue, finish = fetch(NEAR, codes, big, small, kbuf, vbuf, sems)

    def begin(k, _):
        issue(left[k])
        return 0

    def end(k, _):
        finish(left[k])
        return 0

    lax.fori_loop(0, left[SLOTS + RPD - 1], begin, 0)

    def blocks_of(buf, slot, end, count):
        return [
            buf[pl.ds(aligned(jnp.minimum(slot + k, end - 1) * BLOCK), BLOCK), :]
            for k in range(count)
        ]

    def block_row(row, waited):
        lax.fori_loop(waited, left[SLOTS + row], end, 0)
        begin, stop = starts[row], starts[row + 1]
        number = stop - begin
        quads = (number + 1) >> 2
        rest = begin + 4 * quads
        mine = (row >> 2) == core
        local = pl.ds(aligned((row & 3) * BLOCK), BLOCK)
        columns_of = lambda head: slice(head * HEAD_DIM, (head + 1) * HEAD_DIM)
        rows_of = lambda head: slice(head * BLOCK, (head + 1) * BLOCK)

        def take(queries):
            for head in range(HEADS):
                qs[rows_of(head), :] = queries[local, columns_of(head)]

        lax.cond(mine, lambda: take(own_queries), lambda: take(their_queries))
        m_ref[...] = jnp.full(m_ref.shape, -1e30, jnp.float32)
        acc[...] = jnp.zeros(acc.shape, jnp.float32)

        def score(slot, into, count):
            keys = jnp.concatenate(blocks_of(kbuf, slot, stop, count), axis=0)
            scores = SCALE * lax.dot_general(
                qs[...], keys, (((1,), (1,)), ((), ())), preferred_element_type=jnp.float32
            )
            columns = [scores[:, k * BLOCK : (k + 1) * BLOCK] for k in range(count)]
            top = m_ref[...]
            for column in columns:
                top = jnp.maximum(top, column)
            m_ref[...] = top
            columns[-1] = jnp.where(slot + count - 1 < stop, columns[-1], -1e30)
            for k in range(count):
                s_ref[into, :, k * BLOCK : (k + 1) * BLOCK] = columns[k]

        def weigh(slot, into, count):
            values = jnp.concatenate(blocks_of(vbuf, slot, stop, count), axis=0)
            values = jnp.concatenate([values, jnp.ones(values.shape, values.dtype)], axis=1)
            top = m_ref[...]
            weights = jnp.concatenate(
                [
                    jnp.exp2(s_ref[into, :, k * BLOCK : (k + 1) * BLOCK] - top).astype(
                        jnp.bfloat16
                    )
                    for k in range(count)
                ],
                axis=1,
            )
            acc[...] += jnp.dot(weights, values, preferred_element_type=jnp.float32)

        def each_quad(step):
            def body(quad, _):
                step(begin + 4 * quad, quad, 4)
                return 0

            lax.fori_loop(0, quads, body, 0)
            pl.when(rest < stop)(lambda: step(rest, quads, 2))

        each_quad(score)
        m_ref[...] = jnp.broadcast_to(
            jnp.max(m_ref[...], axis=1, keepdims=True), m_ref.shape
        )
        each_quad(weigh)

        lane = lax.broadcasted_iota(jnp.int32, (BLOCK, HEAD_DIM), 1)

        def put(out, stat):
            tile = jnp.zeros((BLOCK, HEAD_DIM), jnp.float32)
            for head in range(HEADS):
                out[local, columns_of(head)] = acc[rows_of(head), :HEAD_DIM].astype(jnp.bfloat16)
                tile = jnp.where(lane == head, m_ref[rows_of(head), :], tile)
                tile = jnp.where(lane == HEADS + head, acc[rows_of(head), HEAD_DIM:], tile)
            stat[local, :] = tile

        lax.cond(mine, lambda: put(own_out, own_stat), lambda: put(their_out, their_stat))
        return left[SLOTS + row]

    lax.fori_loop(0, RPD, block_row, jnp.int32(0))


def attention_call(place, starts, codes, own_queries, their_queries, big, small, listed):
    rows = own_queries.shape[0]
    smem = pl.BlockSpec(memory_space=pltpu.SMEM)
    vmem = pl.BlockSpec(memory_space=pltpu.VMEM)
    hbm = pl.BlockSpec(memory_space=pltpu.HBM)
    keys, values, left = listed
    out = jax.ShapeDtypeStruct((rows, HEADS * HEAD_DIM), jnp.bfloat16)
    stat = jax.ShapeDtypeStruct((rows, HEAD_DIM), jnp.float32)
    blocks = jax.ShapeDtypeStruct(keys.shape, keys.dtype)
    return pl.pallas_call(
        attend,
        name="attend",
        out_shape=(out, stat, out, stat, blocks, blocks),
        in_specs=[*[smem] * 4, vmem, vmem, *[hbm] * 6, vmem, vmem],
        out_specs=(vmem,) * 6,
        input_output_aliases={12: 4, 13: 5},
        scratch_shapes=[
            pltpu.VMEM((HEADS * BLOCK, HEAD_DIM), jnp.bfloat16),
            pltpu.VMEM((QUADS, HEADS * BLOCK, 4 * BLOCK), jnp.float32),
            pltpu.VMEM((HEADS * BLOCK, BLOCK), jnp.float32),
            pltpu.VMEM((HEADS * BLOCK, 2 * HEAD_DIM), jnp.float32),
            pltpu.SemaphoreType.DMA((3, SLOTS)),
        ],
        cost_estimate=pl.CostEstimate(
            flops=8 * SLOTS * HEADS * BLOCK * BLOCK * HEAD_DIM,
            transcendentals=SLOTS * HEADS * BLOCK * BLOCK,
            bytes_accessed=4 * SLOTS * BLOCK * HEAD_DIM + 8 * rows * HEADS * HEAD_DIM,
        ),
        compiler_params=pltpu.CompilerParams(vmem_limit_bytes=20 * 2**20),
    )(
        place,
        starts,
        codes,
        left,
        own_queries,
        their_queries,
        *big[NEAR:],
        *small[NEAR:],
        keys,
        values,
    )[:4]


def project(o_a, stat_a, o_b, stat_b, w_ref, out_ref, att):
    step, tile = pl.program_id(0), out_ref.shape[1]

    def merge(chunk, _):
        rows = pl.ds(aligned(chunk * MERGE), MERGE)
        top_a, top_b = stat_a[rows, :], stat_b[rows, :]
        top = jnp.maximum(top_a, top_b)
        by_a, by_b = jnp.exp2(top_a - top), jnp.exp2(top_b - top)
        sums = lambda stat: pltpu.roll(stat, HEAD_DIM - HEADS, 1)
        total = sums(top_a) * by_a + sums(top_b) * by_b
        by_a, by_b = by_a / total, by_b / total
        for head in range(HEADS):
            columns = slice(head * HEAD_DIM, (head + 1) * HEAD_DIM)
            shape = (MERGE, HEAD_DIM)
            part_a = o_a[rows, columns].astype(jnp.float32) * jnp.broadcast_to(
                by_a[:, head : head + 1], shape
            )
            part_b = o_b[rows, columns].astype(jnp.float32) * jnp.broadcast_to(
                by_b[:, head : head + 1], shape
            )
            att[rows, columns] = (part_a + part_b).astype(jnp.bfloat16)
        return 0

    @pl.when(step == 0)
    def _():
        lax.fori_loop(0, att.shape[0] // MERGE, merge, 0)

    out_ref[...] = jnp.dot(
        att[...],
        w_ref[:, pl.ds(pl.multiple_of(step * tile, 128), tile)],
        preferred_element_type=jnp.float32,
    ).astype(jnp.bfloat16)


def projection_call(o_a, stat_a, o_b, stat_b, w_out):
    rows, depth = o_a.shape
    width, tile = w_out.shape[1], 1024
    vmem = pl.BlockSpec(memory_space=pltpu.VMEM)
    return pl.pallas_call(
        project,
        name="project",
        grid=(width // tile,),
        out_shape=jax.ShapeDtypeStruct((rows, width), jnp.bfloat16),
        in_specs=[vmem] * 5,
        out_specs=pl.BlockSpec((rows, tile), lambda i: (0, i)),
        scratch_shapes=[pltpu.VMEM((rows, depth), jnp.bfloat16)],
        compiler_params=pltpu.CompilerParams(vmem_limit_bytes=30 * 2**20),
    )(o_a, stat_a, o_b, stat_b, w_out)


def tables(row_pos, core, row_ptr, col_blocks):
    ptr = lax.dynamic_slice_in_dim(row_ptr, row_pos * RPD, RPD + 1, 0)
    cols = lax.dynamic_slice_in_dim(col_blocks, row_pos * (RPD * AVG), RPD * AVG, 0)
    starts = (ptr - row_pos * (RPD * AVG) + 1 - core) >> 1
    halves = cols.reshape(-1, 2)
    block = jnp.where(core == 0, halves[:, 0], halves[:, 1]) - 256 * core
    owner, within = block >> 2, block & 3
    mine = {axis: (row_pos // STRIDE[axis]) & 3 for axis in "xyz"}
    theirs = {axis: (owner // STRIDE[axis]) & 3 for axis in "xyz"}
    in_big = jnp.where(
        core == 0, slot_of(theirs, mine, BIG_AXES[0]), slot_of(theirs, mine, BIG_AXES[1])
    )
    in_small = slot_of(theirs, mine, SMALL_AXES[0])

    def piece_and_chunk(place):
        plane, inner = place >> 4, place & 15
        halves = 2 * plane + (inner >> 3)
        thirds = 3 * plane - 2 + ((inner - 4) >> 2) * (inner >> 3)
        whole = (plane < 2) | (inner < 8)
        piece = jnp.where(plane < 2, halves, thirds)
        return piece | jnp.where(whole, inner & 7, inner & 3) << 4

    codes = piece_and_chunk(in_big) | piece_and_chunk(in_small) << 7 | within << 14
    return starts.astype(jnp.int32), codes.astype(jnp.int32)


def local(queries, keys, values, row_ptr, col_blocks, w_out):
    row_pos = lax.axis_index("row")
    core = lax.axis_index("col")
    big, small = gathered(jnp.concatenate([keys, values], axis=0))
    other_queries = swap(queries)
    starts, codes = tables(row_pos, core, row_ptr, col_blocks)
    listed = fetched(codes, starts, big, small)
    own_out, own_stat, their_out, their_stat = attention_call(
        core.reshape(1).astype(jnp.int32),
        starts,
        codes,
        queries,
        other_queries,
        big,
        small,
        listed,
    )
    return projection_call(own_out, own_stat, swap(their_out), swap(their_stat), w_out)


def solution(mesh):
    in_specs = (
        P(("row", "col"), None),
        P(("col", "row"), None),
        P(("col", "row"), None),
        P(),
        P(),
        P(),
    )
    out_specs = P(("row", "col"), None)
    return jax.shard_map(local, mesh=mesh, in_specs=in_specs, out_specs=out_specs, check_vma=False)
```

```python
import jax
import jax.numpy as jnp
from jax import lax
from jax.experimental import pallas as pl
from jax.experimental.pallas import tpu as pltpu
from jax.sharding import PartitionSpec as P

HEADS = 8
HEAD_DIM = 128
BLOCK = 128
RPD = 8
AVG = 16
SHARD = 512
BIG = 672
SMALL = 2 * SHARD - BIG
SPLIT = BIG - SHARD - BLOCK
QUADS = 4
NEAR = 7
MERGE = 64
SLOTS = 64
SCALE = 1.4426950408889634 * HEAD_DIM ** (-0.5)
STRIDE = {"x": 1, "y": 4, "z": 16}
BIG_AXES = ("yzx", "xyz")
SMALL_AXES = ("zxy", "zxy")


def send(array, axes, place):
    pairs = []
    for row in range(64):
        for core in range(2):
            stride = STRIDE[axes[core]]
            at = (row // stride) % 4
            pairs.append((row * 2 + core, (row + (place(at) - at) * stride) * 2 + core))
    return lax.ppermute(array, ("row", "col"), pairs)


def swap(array):
    pairs = [(row * 2 + core, row * 2 + 1 - core) for row in range(64) for core in range(2)]
    return lax.ppermute(array, ("row", "col"), pairs)


def together(*arrays):
    return lax.optimization_barrier(arrays)


def back(array, axes):
    return send(array, axes, lambda at: (at + 3) % 4)


def across(array, axes):
    return send(array, axes, lambda at: (at + 2) % 4)


def forth(array, axes):
    return send(array, axes, lambda at: (at + 1) % 4)


def gathered(both):
    def steps(part, axes):
        first, ring, last = ([axes[core][phase] for core in range(2)] for phase in range(3))
        join = lambda *arrays: jnp.concatenate(arrays, axis=0)
        far, after, before = together(across(part, first), back(part, first), forth(part, first))
        (own,) = together(join(part, after, before, far))
        half = own.shape[0] // 2
        after, before = together(back(own, ring), forth(own, ring))
        first_half, before, low, high = together(
            join(own, after), before, after[:half], before[half:]
        )
        low, high = back(low, ring), forth(high, ring)
        first_after, before_before = back(first_half, last), forth(before, last)
        first_before = forth(first_half, last)
        low, high = together(low, high)
        rest, second = join(low, high), join(before, low, high)
        rest_before = forth(rest, last)
        second_after = back(second, last)
        first_far, before_far = back(first_after, last), forth(before_before, last)
        rest_far = forth(rest_before, last)
        pieces = (
            first_half,
            second,
            first_after,
            second_after,
            first_before,
            before_before,
            rest_before,
            first_far,
            before_far,
            rest_far,
        )
        return [
            pltpu.with_memory_space_constraint(piece.reshape(-1, HEAD_DIM), pltpu.HBM)
            for piece in pieces
        ]

    return (
        steps(both[:BIG].reshape(-1, 8, HEAD_DIM), BIG_AXES),
        steps(both[BIG:].reshape(-1, 8, HEAD_DIM), SMALL_AXES),
    )


def gray(number):
    return number ^ (number >> 1)


def slot_of(theirs, mine, axes):
    first, second, third = axes
    return (
        gray((theirs[first] - mine[first]) & 3)
        + 4 * gray((theirs[second] - mine[second]) & 3)
        + 16 * gray((theirs[third] - mine[third]) & 3)
    )


def choose(number, count, act):
    def between(low, high):
        if high - low == 1:
            act(low)
        else:
            middle = (low + high) // 2
            lax.cond(number < middle, lambda: between(low, middle), lambda: between(middle, high))

    between(0, count)


def aligned(row):
    return pl.multiple_of(row, 16)


def fetch(first_piece, codes, big, small, kbuf, vbuf, sems):
    count = len(big)

    def parts(index):
        code = codes[index]
        big_piece, big_chunk = code & 15, (code >> 4) & 7
        small_piece, small_chunk = (code >> 7) & 15, (code >> 11) & 7
        return big_piece, big_chunk, small_piece, small_chunk, code >> 14, index * BLOCK

    def has(piece):
        return (piece >= first_piece) & (piece < first_piece + count)

    def copy(source, row, rows, target, to, sem):
        return pltpu.make_async_copy(
            source.at[pl.ds(aligned(row), rows), :], target.at[pl.ds(aligned(to), rows), :], sem
        )

    def issue(index):
        big_piece, big_chunk, small_piece, small_chunk, within, at = parts(index)

        def from_big(piece):
            row = big_chunk * BIG
            copy(big[piece], row + within * BLOCK, BLOCK, kbuf, at, sems.at[index]).start()

            @pl.when(within == 0)
            def _():
                copy(big[piece], row + SHARD, BLOCK, vbuf, at, sems.at[index]).start()

            @pl.when(within == 1)
            def _():
                copy(big[piece], row + SHARD + BLOCK, SPLIT, vbuf, at, sems.at[index]).start()

        def from_small(piece):
            row = small_chunk * SMALL

            @pl.when(within == 1)
            def _():
                copy(small[piece], row, BLOCK - SPLIT, vbuf, at + SPLIT, sems.at[index]).start()

            @pl.when(within >= 2)
            def _():
                copy(
                    small[piece],
                    row + BLOCK - SPLIT + (within - 2) * BLOCK,
                    BLOCK,
                    vbuf,
                    at,
                    sems.at[index],
                ).start()

        pl.when(has(big_piece))(lambda: choose(big_piece - first_piece, count, from_big))
        pl.when(has(small_piece) & (within >= 1))(
            lambda: choose(small_piece - first_piece, count, from_small)
        )

    def finish(index):
        big_piece, _, small_piece, _, within, _ = parts(index)
        from_big = BLOCK + jnp.where(within == 0, BLOCK, jnp.where(within == 1, SPLIT, 0))
        from_small = jnp.where(within == 0, 0, jnp.where(within == 1, BLOCK - SPLIT, BLOCK))
        rows = jnp.where(has(big_piece), from_big, 0) + jnp.where(has(small_piece), from_small, 0)
        for number in sorted({BLOCK - SPLIT, BLOCK, BLOCK + SPLIT, 2 * BLOCK}):

            @pl.when(rows == number)
            def _():
                copy(big[1], 0, number, kbuf, 0, sems.at[index]).wait()

    return parts, has, issue, finish


def fetch_near(codes, starts, *refs):
    big, small = refs[:NEAR], refs[NEAR : 2 * NEAR]
    kbuf, vbuf, left, sems = refs[2 * NEAR :]
    parts, has, issue, finish = fetch(0, codes, big, small, kbuf, vbuf, sems)

    def begin(index, missing):
        issue(index)
        big_piece, _, small_piece, _, within, _ = parts(index)
        left[missing] = index
        whole = has(big_piece) & (has(small_piece) | (within == 0))
        return missing + jnp.where(whole, jnp.int32(0), jnp.int32(1))

    def block_row(row, missing):
        missing = lax.fori_loop(starts[row], starts[row + 1], begin, missing)
        left[SLOTS + row] = missing
        return missing

    def end(index, _):
        finish(index)
        return 0

    lax.fori_loop(0, RPD, block_row, jnp.int32(0))
    lax.fori_loop(0, SLOTS, end, 0)


def fetched(codes, starts, big, small):
    vmem = pl.BlockSpec(memory_space=pltpu.VMEM)
    smem = pl.BlockSpec(memory_space=pltpu.SMEM)
    hbm = pl.BlockSpec(memory_space=pltpu.HBM)
    blocks = jax.ShapeDtypeStruct((SLOTS * BLOCK, HEAD_DIM), jnp.bfloat16)
    return pl.pallas_call(
        fetch_near,
        name="fetch_near",
        in_specs=[smem, smem, *[hbm] * (2 * NEAR)],
        out_shape=(blocks, blocks, jax.ShapeDtypeStruct((2 * SLOTS,), jnp.int32)),
        out_specs=(vmem, vmem, smem),
        scratch_shapes=[pltpu.SemaphoreType.DMA((SLOTS,))],
        compiler_params=pltpu.CompilerParams(vmem_limit_bytes=10 * 2**20),
    )(codes, starts, *big[:NEAR], *small[:NEAR])


def attend(place, starts, codes, left, own_queries, their_queries, *refs):
    big, small = refs[:3], refs[3:6]
    own_out, own_stat, their_out, their_stat, kbuf, vbuf = refs[8:14]
    qs, s_ref, m_ref, acc, sems = refs[14:]
    core = place[0]
    _, _, issue, finish = fetch(NEAR, codes, big, small, kbuf, vbuf, sems)

    def begin(k, _):
        issue(left[k])
        return 0

    def end(k, _):
        finish(left[k])
        return 0

    lax.fori_loop(0, left[SLOTS + RPD - 1], begin, 0)

    def blocks_of(buf, slot, end, count):
        return [
            buf[pl.ds(aligned(jnp.minimum(slot + k, end - 1) * BLOCK), BLOCK), :]
            for k in range(count)
        ]

    def block_row(row, waited):
        lax.fori_loop(waited, left[SLOTS + row], end, 0)
        begin, stop = starts[row], starts[row + 1]
        number = stop - begin
        quads = (number + 1) >> 2
        rest = begin + 4 * quads
        mine = (row >> 2) == core
        local = pl.ds(aligned((row & 3) * BLOCK), BLOCK)
        columns_of = lambda head: slice(head * HEAD_DIM, (head + 1) * HEAD_DIM)
        rows_of = lambda head: slice(head * BLOCK, (head + 1) * BLOCK)

        def take(queries):
            for head in range(HEADS):
                qs[rows_of(head), :] = queries[local, columns_of(head)]

        lax.cond(mine, lambda: take(own_queries), lambda: take(their_queries))

        @pl.when(number == 0)
        def _():
            m_ref[...] = jnp.full(m_ref.shape, -1e30, jnp.float32)
            acc[...] = jnp.zeros(acc.shape, jnp.float32)


        def score(slot, into, count):
            keys = jnp.concatenate(blocks_of(kbuf, slot, stop, count), axis=0)
            scores = SCALE * lax.dot_general(
                qs[...], keys, (((1,), (1,)), ((), ())), preferred_element_type=jnp.float32
            )
            columns = [scores[:, k * BLOCK : (k + 1) * BLOCK] for k in range(count)]
            top = jnp.where(slot == begin, -1e30, m_ref[...])
            for column in columns:
                top = jnp.maximum(top, column)
            m_ref[...] = top
            columns[-1] = jnp.where(slot + count - 1 < stop, columns[-1], -1e30)
            for k in range(count):
                s_ref[into, :, k * BLOCK : (k + 1) * BLOCK] = columns[k]

        def weigh(slot, into, count):
            values = jnp.concatenate(blocks_of(vbuf, slot, stop, count), axis=0)
            values = jnp.concatenate([values, jnp.ones(values.shape, values.dtype)], axis=1)
            top = m_ref[...]
            weights = jnp.concatenate(
                [
                    jnp.exp2(s_ref[into, :, k * BLOCK : (k + 1) * BLOCK] - top).astype(
                        jnp.bfloat16
                    )
                    for k in range(count)
                ],
                axis=1,
            )
            before = jnp.where(slot == begin, 0.0, acc[...])
            acc[...] = before + jnp.dot(weights, values, preferred_element_type=jnp.float32)

        def each_quad(step):
            def body(quad, _):
                step(begin + 4 * quad, quad, 4)
                return 0

            lax.fori_loop(0, quads, body, 0)
            pl.when(rest < stop)(lambda: step(rest, quads, 2))

        each_quad(score)
        m_ref[...] = jnp.broadcast_to(
            jnp.max(m_ref[...], axis=1, keepdims=True), m_ref.shape
        )
        each_quad(weigh)

        lane = lax.broadcasted_iota(jnp.int32, (BLOCK, HEAD_DIM), 1)

        def put(out, stat):
            tile = jnp.zeros((BLOCK, HEAD_DIM), jnp.float32)
            for head in range(HEADS):
                out[local, columns_of(head)] = acc[rows_of(head), :HEAD_DIM].astype(jnp.bfloat16)
                tile = jnp.where(lane == head, m_ref[rows_of(head), :], tile)
                tile = jnp.where(lane == HEADS + head, acc[rows_of(head), HEAD_DIM:], tile)
            stat[local, :] = tile

        lax.cond(mine, lambda: put(own_out, own_stat), lambda: put(their_out, their_stat))
        return left[SLOTS + row]

    lax.fori_loop(0, RPD, block_row, jnp.int32(0))


def attention_call(place, starts, codes, own_queries, their_queries, big, small, listed):
    rows = own_queries.shape[0]
    smem = pl.BlockSpec(memory_space=pltpu.SMEM)
    vmem = pl.BlockSpec(memory_space=pltpu.VMEM)
    hbm = pl.BlockSpec(memory_space=pltpu.HBM)
    keys, values, left = listed
    out = jax.ShapeDtypeStruct((rows, HEADS * HEAD_DIM), jnp.bfloat16)
    stat = jax.ShapeDtypeStruct((rows, HEAD_DIM), jnp.float32)
    blocks = jax.ShapeDtypeStruct(keys.shape, keys.dtype)
    return pl.pallas_call(
        attend,
        name="attend",
        out_shape=(out, stat, out, stat, blocks, blocks),
        in_specs=[*[smem] * 4, vmem, vmem, *[hbm] * 6, vmem, vmem],
        out_specs=(vmem,) * 6,
        input_output_aliases={12: 4, 13: 5},
        scratch_shapes=[
            pltpu.VMEM((HEADS * BLOCK, HEAD_DIM), jnp.bfloat16),
            pltpu.VMEM((QUADS, HEADS * BLOCK, 4 * BLOCK), jnp.float32),
            pltpu.VMEM((HEADS * BLOCK, BLOCK), jnp.float32),
            pltpu.VMEM((HEADS * BLOCK, 2 * HEAD_DIM), jnp.float32),
            pltpu.SemaphoreType.DMA((SLOTS,)),
        ],
        cost_estimate=pl.CostEstimate(
            flops=8 * SLOTS * HEADS * BLOCK * BLOCK * HEAD_DIM,
            transcendentals=SLOTS * HEADS * BLOCK * BLOCK,
            bytes_accessed=4 * SLOTS * BLOCK * HEAD_DIM + 8 * rows * HEADS * HEAD_DIM,
        ),
        compiler_params=pltpu.CompilerParams(vmem_limit_bytes=20 * 2**20),
    )(
        place,
        starts,
        codes,
        left,
        own_queries,
        their_queries,
        *big[NEAR:],
        *small[NEAR:],
        keys,
        values,
    )[:4]


def project(o_a, stat_a, o_b, stat_b, w_ref, out_ref, att):
    step, tile = pl.program_id(0), out_ref.shape[1]

    def merge(chunk, _):
        rows = pl.ds(aligned(chunk * MERGE), MERGE)
        top_a, top_b = stat_a[rows, :], stat_b[rows, :]
        top = jnp.maximum(top_a, top_b)
        by_a, by_b = jnp.exp2(top_a - top), jnp.exp2(top_b - top)
        sums = lambda stat: pltpu.roll(stat, HEAD_DIM - HEADS, 1)
        total = sums(top_a) * by_a + sums(top_b) * by_b
        by_a, by_b = by_a / total, by_b / total
        for head in range(HEADS):
            columns = slice(head * HEAD_DIM, (head + 1) * HEAD_DIM)
            shape = (MERGE, HEAD_DIM)
            part_a = o_a[rows, columns].astype(jnp.float32) * jnp.broadcast_to(
                by_a[:, head : head + 1], shape
            )
            part_b = o_b[rows, columns].astype(jnp.float32) * jnp.broadcast_to(
                by_b[:, head : head + 1], shape
            )
            att[rows, columns] = (part_a + part_b).astype(jnp.bfloat16)
        return 0

    @pl.when(step == 0)
    def _():
        lax.fori_loop(0, att.shape[0] // MERGE, merge, 0)

    out_ref[...] = jnp.dot(
        att[...],
        w_ref[:, pl.ds(pl.multiple_of(step * tile, 128), tile)],
        preferred_element_type=jnp.float32,
    ).astype(jnp.bfloat16)


def projection_call(o_a, stat_a, o_b, stat_b, w_out):
    rows, depth = o_a.shape
    width, tile = w_out.shape[1], 1024
    vmem = pl.BlockSpec(memory_space=pltpu.VMEM)
    return pl.pallas_call(
        project,
        name="project",
        grid=(width // tile,),
        out_shape=jax.ShapeDtypeStruct((rows, width), jnp.bfloat16),
        in_specs=[vmem] * 5,
        out_specs=pl.BlockSpec((rows, tile), lambda i: (0, i)),
        scratch_shapes=[pltpu.VMEM((rows, depth), jnp.bfloat16)],
        compiler_params=pltpu.CompilerParams(vmem_limit_bytes=30 * 2**20),
    )(o_a, stat_a, o_b, stat_b, w_out)


def tables(row_pos, core, row_ptr, col_blocks):
    ptr = lax.dynamic_slice_in_dim(row_ptr, row_pos * RPD, RPD + 1, 0)
    cols = lax.dynamic_slice_in_dim(col_blocks, row_pos * (RPD * AVG), RPD * AVG, 0)
    starts = (ptr - row_pos * (RPD * AVG) + 1 - core) >> 1
    halves = cols.reshape(-1, 2)
    block = jnp.where(core == 0, halves[:, 0], halves[:, 1]) - 256 * core
    owner, within = block >> 2, block & 3
    mine = {axis: (row_pos // STRIDE[axis]) & 3 for axis in "xyz"}
    theirs = {axis: (owner // STRIDE[axis]) & 3 for axis in "xyz"}
    in_big = jnp.where(
        core == 0, slot_of(theirs, mine, BIG_AXES[0]), slot_of(theirs, mine, BIG_AXES[1])
    )
    in_small = slot_of(theirs, mine, SMALL_AXES[0])

    def piece_and_chunk(place):
        plane, inner = place >> 4, place & 15
        halves = 2 * plane + (inner >> 3)
        thirds = 3 * plane - 2 + ((inner - 4) >> 2) * (inner >> 3)
        whole = (plane < 2) | (inner < 8)
        piece = jnp.where(plane < 2, halves, thirds)
        return piece | jnp.where(whole, inner & 7, inner & 3) << 4

    codes = piece_and_chunk(in_big) | piece_and_chunk(in_small) << 7 | within << 14
    return starts.astype(jnp.int32), codes.astype(jnp.int32)


def local(queries, keys, values, row_ptr, col_blocks, w_out):
    row_pos = lax.axis_index("row")
    core = lax.axis_index("col")
    big, small = gathered(jnp.concatenate([keys, values], axis=0))
    other_queries = swap(queries)
    starts, codes = tables(row_pos, core, row_ptr, col_blocks)
    listed = fetched(codes, starts, big, small)
    own_out, own_stat, their_out, their_stat = attention_call(
        core.reshape(1).astype(jnp.int32),
        starts,
        codes,
        queries,
        other_queries,
        big,
        small,
        listed,
    )
    return projection_call(own_out, own_stat, swap(their_out), swap(their_stat), w_out)


def solution(mesh):
    in_specs = (
        P(("row", "col"), None),
        P(("col", "row"), None),
        P(("col", "row"), None),
        P(),
        P(),
        P(),
    )
    out_specs = P(("row", "col"), None)
    return jax.shard_map(local, mesh=mesh, in_specs=in_specs, out_specs=out_specs, check_vma=False)
```

```python
import jax
import jax.numpy as jnp
from jax import lax
from jax.experimental import pallas as pl
from jax.experimental.pallas import tpu as pltpu
from jax.sharding import PartitionSpec as P

HEADS = 8
HEAD_DIM = 128
BLOCK = 128
RPD = 8
AVG = 16
SHARD = 512
BIG = 672
SMALL = 2 * SHARD - BIG
SPLIT = BIG - SHARD - BLOCK
QUADS = 4
NEAR = 7
MERGE = 64
SLOTS = 64
SCALE = 1.4426950408889634 * HEAD_DIM ** (-0.5)
STRIDE = {"x": 1, "y": 4, "z": 16}
BIG_AXES = ("yzx", "xyz")
SMALL_AXES = ("zxy", "zxy")


def send(array, axes, place):
    pairs = []
    for row in range(64):
        for core in range(2):
            stride = STRIDE[axes[core]]
            at = (row // stride) % 4
            pairs.append((row * 2 + core, (row + (place(at) - at) * stride) * 2 + core))
    return lax.ppermute(array, ("row", "col"), pairs)


def swap(array):
    pairs = [(row * 2 + core, row * 2 + 1 - core) for row in range(64) for core in range(2)]
    return lax.ppermute(array, ("row", "col"), pairs)


def together(*arrays):
    return lax.optimization_barrier(arrays)


def back(array, axes):
    return send(array, axes, lambda at: (at + 3) % 4)


def across(array, axes):
    return send(array, axes, lambda at: (at + 2) % 4)


def forth(array, axes):
    return send(array, axes, lambda at: (at + 1) % 4)


def gathered(both):
    def steps(part, axes):
        first, ring, last = ([axes[core][phase] for core in range(2)] for phase in range(3))
        join = lambda *arrays: jnp.concatenate(arrays, axis=0)
        far, after, before = together(across(part, first), back(part, first), forth(part, first))
        (own,) = together(join(part, after, before, far))
        half = own.shape[0] // 2
        after, before = together(back(own, ring), forth(own, ring))
        first_half, before, low, high = together(
            join(own, after), before, after[:half], before[half:]
        )
        low, high = back(low, ring), forth(high, ring)
        first_after = back(first_half, last)
        before_before = forth(before, last)
        first_before = forth(first_half, last)
        low, high, kept = together(low, high, before)
        rest, second = join(low, high), join(kept, low, high)
        rest_before = forth(rest, last)
        second_after = back(second, last)
        first_far, before_far = back(first_after, last), forth(before_before, last)
        rest_far = forth(rest_before, last)
        pieces = (
            first_half,
            second,
            first_after,
            second_after,
            first_before,
            before_before,
            rest_before,
            first_far,
            before_far,
            rest_far,
        )
        return [
            pltpu.with_memory_space_constraint(piece.reshape(-1, HEAD_DIM), pltpu.HBM)
            for piece in pieces
        ]

    return (
        steps(both[:BIG].reshape(-1, 8, HEAD_DIM), BIG_AXES),
        steps(both[BIG:].reshape(-1, 8, HEAD_DIM), SMALL_AXES),
    )


def gray(number):
    return number ^ (number >> 1)


def slot_of(theirs, mine, axes):
    first, second, third = axes
    return (
        gray((theirs[first] - mine[first]) & 3)
        + 4 * gray((theirs[second] - mine[second]) & 3)
        + 16 * gray((theirs[third] - mine[third]) & 3)
    )


def choose(number, count, act):
    def between(low, high):
        if high - low == 1:
            act(low)
        else:
            middle = (low + high) // 2
            lax.cond(number < middle, lambda: between(low, middle), lambda: between(middle, high))

    between(0, count)


def aligned(row):
    return pl.multiple_of(row, 16)


def fetch(first_piece, codes, big, small, kbuf, vbuf, sems):
    count = len(big)

    def parts(index):
        code = codes[index]
        big_piece, big_chunk = code & 15, (code >> 4) & 7
        small_piece, small_chunk = (code >> 7) & 15, (code >> 11) & 7
        return big_piece, big_chunk, small_piece, small_chunk, code >> 14, index * BLOCK

    def has(piece):
        return (piece >= first_piece) & (piece < first_piece + count)

    def copy(source, row, rows, target, to, sem):
        return pltpu.make_async_copy(
            source.at[pl.ds(aligned(row), rows), :], target.at[pl.ds(aligned(to), rows), :], sem
        )

    def issue(index):
        big_piece, big_chunk, small_piece, small_chunk, within, at = parts(index)

        def from_big(piece):
            row = big_chunk * BIG
            copy(big[piece], row + within * BLOCK, BLOCK, kbuf, at, sems.at[index]).start()

            @pl.when(within == 0)
            def _():
                copy(big[piece], row + SHARD, BLOCK, vbuf, at, sems.at[index]).start()

            @pl.when(within == 1)
            def _():
                copy(big[piece], row + SHARD + BLOCK, SPLIT, vbuf, at, sems.at[index]).start()

        def from_small(piece):
            row = small_chunk * SMALL

            @pl.when(within == 1)
            def _():
                copy(small[piece], row, BLOCK - SPLIT, vbuf, at + SPLIT, sems.at[index]).start()

            @pl.when(within >= 2)
            def _():
                copy(
                    small[piece],
                    row + BLOCK - SPLIT + (within - 2) * BLOCK,
                    BLOCK,
                    vbuf,
                    at,
                    sems.at[index],
                ).start()

        pl.when(has(big_piece))(lambda: choose(big_piece - first_piece, count, from_big))
        pl.when(has(small_piece) & (within >= 1))(
            lambda: choose(small_piece - first_piece, count, from_small)
        )

    def finish(index):
        big_piece, _, small_piece, _, within, _ = parts(index)
        from_big = BLOCK + jnp.where(within == 0, BLOCK, jnp.where(within == 1, SPLIT, 0))
        from_small = jnp.where(within == 0, 0, jnp.where(within == 1, BLOCK - SPLIT, BLOCK))
        rows = jnp.where(has(big_piece), from_big, 0) + jnp.where(has(small_piece), from_small, 0)
        for number in sorted({BLOCK - SPLIT, BLOCK, BLOCK + SPLIT, 2 * BLOCK}):

            @pl.when(rows == number)
            def _():
                copy(big[1], 0, number, kbuf, 0, sems.at[index]).wait()

    return parts, has, issue, finish


def fetch_near(codes, starts, *refs):
    big, small = refs[:NEAR], refs[NEAR : 2 * NEAR]
    kbuf, vbuf, left, sems = refs[2 * NEAR :]
    parts, has, issue, finish = fetch(0, codes, big, small, kbuf, vbuf, sems)

    def begin(index, missing):
        issue(index)
        big_piece, _, small_piece, _, within, _ = parts(index)
        left[missing] = index
        whole = has(big_piece) & (has(small_piece) | (within == 0))
        return missing + jnp.where(whole, jnp.int32(0), jnp.int32(1))

    def block_row(row, missing):
        missing = lax.fori_loop(starts[row], starts[row + 1], begin, missing)
        left[SLOTS + row] = missing
        return missing

    def end(index, _):
        finish(index)
        return 0

    lax.fori_loop(0, RPD, block_row, jnp.int32(0))
    lax.fori_loop(0, SLOTS, end, 0)


def fetched(codes, starts, big, small):
    vmem = pl.BlockSpec(memory_space=pltpu.VMEM)
    smem = pl.BlockSpec(memory_space=pltpu.SMEM)
    hbm = pl.BlockSpec(memory_space=pltpu.HBM)
    blocks = jax.ShapeDtypeStruct((SLOTS * BLOCK, HEAD_DIM), jnp.bfloat16)
    return pl.pallas_call(
        fetch_near,
        name="fetch_near",
        in_specs=[smem, smem, *[hbm] * (2 * NEAR)],
        out_shape=(blocks, blocks, jax.ShapeDtypeStruct((2 * SLOTS,), jnp.int32)),
        out_specs=(vmem, vmem, smem),
        scratch_shapes=[pltpu.SemaphoreType.DMA((SLOTS,))],
        compiler_params=pltpu.CompilerParams(vmem_limit_bytes=10 * 2**20),
    )(codes, starts, *big[:NEAR], *small[:NEAR])


def attend(place, starts, codes, left, own_queries, their_queries, *refs):
    big, small = refs[:3], refs[3:6]
    own_out, own_stat, their_out, their_stat, kbuf, vbuf = refs[8:14]
    qs, s_ref, m_ref, acc, sems = refs[14:]
    core = place[0]
    _, _, issue, finish = fetch(NEAR, codes, big, small, kbuf, vbuf, sems)

    def begin(k, _):
        issue(left[k])
        return 0

    def end(k, _):
        finish(left[k])
        return 0

    lax.fori_loop(0, left[SLOTS + RPD - 1], begin, 0)

    def blocks_of(buf, slot, end, count):
        return [
            buf[pl.ds(aligned(jnp.minimum(slot + k, end - 1) * BLOCK), BLOCK), :]
            for k in range(count)
        ]

    def block_row(row, waited):
        lax.fori_loop(waited, left[SLOTS + row], end, 0)
        begin, stop = starts[row], starts[row + 1]
        number = stop - begin
        quads = (number + 1) >> 2
        rest = begin + 4 * quads
        mine = (row >> 2) == core
        local = pl.ds(aligned((row & 3) * BLOCK), BLOCK)
        columns_of = lambda head: slice(head * HEAD_DIM, (head + 1) * HEAD_DIM)
        rows_of = lambda head: slice(head * BLOCK, (head + 1) * BLOCK)

        def take(queries):
            for head in range(HEADS):
                qs[rows_of(head), :] = queries[local, columns_of(head)]

        lax.cond(mine, lambda: take(own_queries), lambda: take(their_queries))

        @pl.when(number == 0)
        def _():
            m_ref[...] = jnp.full(m_ref.shape, -1e30, jnp.float32)
            acc[...] = jnp.zeros(acc.shape, jnp.float32)


        def score(slot, into, count):
            keys = jnp.concatenate(blocks_of(kbuf, slot, stop, count), axis=0)
            scores = SCALE * lax.dot_general(
                qs[...], keys, (((1,), (1,)), ((), ())), preferred_element_type=jnp.float32
            )
            columns = [scores[:, k * BLOCK : (k + 1) * BLOCK] for k in range(count)]
            top = jnp.where(slot == begin, -1e30, m_ref[...])
            for column in columns:
                top = jnp.maximum(top, column)
            m_ref[...] = top
            columns[-1] = jnp.where(slot + count - 1 < stop, columns[-1], -1e30)
            for k in range(count):
                s_ref[into, :, k * BLOCK : (k + 1) * BLOCK] = columns[k]

        def weigh(slot, into, count):
            values = jnp.concatenate(blocks_of(vbuf, slot, stop, count), axis=0)
            values = jnp.concatenate([values, jnp.ones(values.shape, values.dtype)], axis=1)
            top = m_ref[...]
            weights = jnp.concatenate(
                [
                    jnp.exp2(s_ref[into, :, k * BLOCK : (k + 1) * BLOCK] - top).astype(
                        jnp.bfloat16
                    )
                    for k in range(count)
                ],
                axis=1,
            )
            before = jnp.where(slot == begin, 0.0, acc[...])
            acc[...] = before + jnp.dot(weights, values, preferred_element_type=jnp.float32)

        def each_quad(step):
            def body(quad, _):
                step(begin + 4 * quad, quad, 4)
                return 0

            lax.fori_loop(0, quads, body, 0)
            pl.when(rest < stop)(lambda: step(rest, quads, 2))

        each_quad(score)
        m_ref[...] = jnp.broadcast_to(
            jnp.max(m_ref[...], axis=1, keepdims=True), m_ref.shape
        )
        each_quad(weigh)

        lane = lax.broadcasted_iota(jnp.int32, (BLOCK, HEAD_DIM), 1)

        def put(out, stat):
            tile = jnp.zeros((BLOCK, HEAD_DIM), jnp.float32)
            for head in range(HEADS):
                out[local, columns_of(head)] = acc[rows_of(head), :HEAD_DIM].astype(jnp.bfloat16)
                tile = jnp.where(lane == head, m_ref[rows_of(head), :], tile)
                tile = jnp.where(lane == HEADS + head, acc[rows_of(head), HEAD_DIM:], tile)
            stat[local, :] = tile

        lax.cond(mine, lambda: put(own_out, own_stat), lambda: put(their_out, their_stat))
        return left[SLOTS + row]

    lax.fori_loop(0, RPD, block_row, jnp.int32(0))


def attention_call(place, starts, codes, own_queries, their_queries, big, small, listed):
    rows = own_queries.shape[0]
    smem = pl.BlockSpec(memory_space=pltpu.SMEM)
    vmem = pl.BlockSpec(memory_space=pltpu.VMEM)
    hbm = pl.BlockSpec(memory_space=pltpu.HBM)
    keys, values, left = listed
    out = jax.ShapeDtypeStruct((rows, HEADS * HEAD_DIM), jnp.bfloat16)
    stat = jax.ShapeDtypeStruct((rows, HEAD_DIM), jnp.float32)
    blocks = jax.ShapeDtypeStruct(keys.shape, keys.dtype)
    return pl.pallas_call(
        attend,
        name="attend",
        out_shape=(out, stat, out, stat, blocks, blocks),
        in_specs=[*[smem] * 4, vmem, vmem, *[hbm] * 6, vmem, vmem],
        out_specs=(vmem,) * 6,
        input_output_aliases={12: 4, 13: 5},
        scratch_shapes=[
            pltpu.VMEM((HEADS * BLOCK, HEAD_DIM), jnp.bfloat16),
            pltpu.VMEM((QUADS, HEADS * BLOCK, 4 * BLOCK), jnp.float32),
            pltpu.VMEM((HEADS * BLOCK, BLOCK), jnp.float32),
            pltpu.VMEM((HEADS * BLOCK, 2 * HEAD_DIM), jnp.float32),
            pltpu.SemaphoreType.DMA((SLOTS,)),
        ],
        cost_estimate=pl.CostEstimate(
            flops=8 * SLOTS * HEADS * BLOCK * BLOCK * HEAD_DIM,
            transcendentals=SLOTS * HEADS * BLOCK * BLOCK,
            bytes_accessed=4 * SLOTS * BLOCK * HEAD_DIM + 8 * rows * HEADS * HEAD_DIM,
        ),
        compiler_params=pltpu.CompilerParams(vmem_limit_bytes=20 * 2**20),
    )(
        place,
        starts,
        codes,
        left,
        own_queries,
        their_queries,
        *big[NEAR:],
        *small[NEAR:],
        keys,
        values,
    )[:4]


def project(o_a, stat_a, o_b, stat_b, w_ref, out_ref, att):
    step, tile = pl.program_id(0), out_ref.shape[1]

    def merge(chunk, _):
        rows = pl.ds(aligned(chunk * MERGE), MERGE)
        top_a, top_b = stat_a[rows, :], stat_b[rows, :]
        top = jnp.maximum(top_a, top_b)
        by_a, by_b = jnp.exp2(top_a - top), jnp.exp2(top_b - top)
        sums = lambda stat: pltpu.roll(stat, HEAD_DIM - HEADS, 1)
        total = sums(top_a) * by_a + sums(top_b) * by_b
        by_a, by_b = by_a / total, by_b / total
        for head in range(HEADS):
            columns = slice(head * HEAD_DIM, (head + 1) * HEAD_DIM)
            shape = (MERGE, HEAD_DIM)
            part_a = o_a[rows, columns].astype(jnp.float32) * jnp.broadcast_to(
                by_a[:, head : head + 1], shape
            )
            part_b = o_b[rows, columns].astype(jnp.float32) * jnp.broadcast_to(
                by_b[:, head : head + 1], shape
            )
            att[rows, columns] = (part_a + part_b).astype(jnp.bfloat16)
        return 0

    @pl.when(step == 0)
    def _():
        lax.fori_loop(0, att.shape[0] // MERGE, merge, 0)

    out_ref[...] = jnp.dot(
        att[...],
        w_ref[:, pl.ds(pl.multiple_of(step * tile, 128), tile)],
        preferred_element_type=jnp.float32,
    ).astype(jnp.bfloat16)


def projection_call(o_a, stat_a, o_b, stat_b, w_out):
    rows, depth = o_a.shape
    width, tile = w_out.shape[1], 1024
    vmem = pl.BlockSpec(memory_space=pltpu.VMEM)
    return pl.pallas_call(
        project,
        name="project",
        grid=(width // tile,),
        out_shape=jax.ShapeDtypeStruct((rows, width), jnp.bfloat16),
        in_specs=[vmem] * 5,
        out_specs=pl.BlockSpec((rows, tile), lambda i: (0, i)),
        scratch_shapes=[pltpu.VMEM((rows, depth), jnp.bfloat16)],
        compiler_params=pltpu.CompilerParams(vmem_limit_bytes=30 * 2**20),
    )(o_a, stat_a, o_b, stat_b, w_out)


def tables(row_pos, core, row_ptr, col_blocks):
    ptr = lax.dynamic_slice_in_dim(row_ptr, row_pos * RPD, RPD + 1, 0)
    cols = lax.dynamic_slice_in_dim(col_blocks, row_pos * (RPD * AVG), RPD * AVG, 0)
    starts = (ptr - row_pos * (RPD * AVG) + 1 - core) >> 1
    halves = cols.reshape(-1, 2)
    block = jnp.where(core == 0, halves[:, 0], halves[:, 1]) - 256 * core
    owner, within = block >> 2, block & 3
    mine = {axis: (row_pos // STRIDE[axis]) & 3 for axis in "xyz"}
    theirs = {axis: (owner // STRIDE[axis]) & 3 for axis in "xyz"}
    in_big = jnp.where(
        core == 0, slot_of(theirs, mine, BIG_AXES[0]), slot_of(theirs, mine, BIG_AXES[1])
    )
    in_small = slot_of(theirs, mine, SMALL_AXES[0])

    def piece_and_chunk(place):
        plane, inner = place >> 4, place & 15
        halves = 2 * plane + (inner >> 3)
        thirds = 3 * plane - 2 + ((inner - 4) >> 2) * (inner >> 3)
        whole = (plane < 2) | (inner < 8)
        piece = jnp.where(plane < 2, halves, thirds)
        return piece | jnp.where(whole, inner & 7, inner & 3) << 4

    codes = piece_and_chunk(in_big) | piece_and_chunk(in_small) << 7 | within << 14
    return starts.astype(jnp.int32), codes.astype(jnp.int32)


def local(queries, keys, values, row_ptr, col_blocks, w_out):
    row_pos = lax.axis_index("row")
    core = lax.axis_index("col")
    big, small = gathered(jnp.concatenate([keys, values], axis=0))
    other_queries = swap(queries)
    starts, codes = tables(row_pos, core, row_ptr, col_blocks)
    listed = fetched(codes, starts, big, small)
    own_out, own_stat, their_out, their_stat = attention_call(
        core.reshape(1).astype(jnp.int32),
        starts,
        codes,
        queries,
        other_queries,
        big,
        small,
        listed,
    )
    return projection_call(own_out, own_stat, swap(their_out), swap(their_stat), w_out)


def solution(mesh):
    in_specs = (
        P(("row", "col"), None),
        P(("col", "row"), None),
        P(("col", "row"), None),
        P(),
        P(),
        P(),
    )
    out_specs = P(("row", "col"), None)
    return jax.shard_map(local, mesh=mesh, in_specs=in_specs, out_specs=out_specs, check_vma=False)
```
